1024 devices in a mesh: mem: 16 (over z, x_lo), rows: 64 (over y, x_hi, core).
Axes of the slice: x: 8 (x_hi: 4, x_lo: 2; x = x_hi * 2 + x_lo), y: 8, z: 8, core: 2. Of those that a mesh axis runs over, the one named last changes fastest.
Arguments:
- sample_collection: float32 [256, 2, 512, 128], P('mem', None, 'rows'), may hold values from -6 to 6
- obs_values: float32 [2, 512, 128], P(None, 'rows', 'mem'), may hold values from -6 to 6
- obs_inverse_variance: float32 [2, 512, 128], P(None, 'rows', 'mem'), may hold values from 0.5 to 4
- obs_mask: int32 [2, 512, 128], P(None, 'rows', 'mem'), may hold values 0 or 1
Outputs:
- cycled: float32 [256, 2, 512, 128], P('mem', None, 'rows')
The draws below stay inside these ranges and needn't reach their ends.
All inputs are finite; a program needn't handle non-finite values. No bound on the sum of `obs_mask` on one device may be relied on, other than what follows from the above.
Results may differ from the reference program's by a relative error of at most 0.0051.
Values may be sent and summed in bfloat16 or wider, within the bound.
A program may use at most 32 MiB of HBM per device.

```python
import math
import jax
import jax.numpy as jnp
from jax import lax

MEMBERS = 256
PATCH = 8
RADIUS = 4
FSTEPS = 4
SCHULZ_STEPS = 3
NY = 512
NX = 128


def with_ends(values, own_key, least, high):
    spot = [jax.random.randint(jax.random.fold_in(own_key, axis), (), 0, length) for axis, length in enumerate(values.shape)]
    longest = values.shape.index(max(values.shape))
    neighbour = spot[:longest] + [(spot[longest] + 1) % values.shape[longest]] + spot[longest + 1:]
    return values.at[tuple(spot)].set(least).at[tuple(neighbour)].set(high)


def steps_of(rng, shape, cuts, least, top_value):
    loudness, own = 1.0, jax.random.fold_in(rng, 6)
    for dim, parts in cuts:
        heights = jnp.exp(jax.random.uniform(jax.random.fold_in(own, dim), (parts,), jnp.float32, least / len(cuts), top_value / len(cuts)))
        loudness = loudness * jnp.repeat(heights, shape[dim] // parts).reshape([-1 if axis == dim else 1 for axis in range(len(shape))])
    return loudness


def gaussian(stream_key, extent, scale, bound, shards=(), kind=jnp.bfloat16):
    result = scale * jax.random.normal(stream_key, extent, jnp.float32)
    if shards:
        result = result * steps_of(stream_key, extent, shards, -0.22, 0.18)
    return jnp.clip(result, -bound, bound).astype(kind)


def setup_inputs(seed: int = 0) -> dict:
    streams_of = jax.random.split(jax.random.key(seed), 5)
    sample_collection = gaussian(streams_of[0], (MEMBERS, 2, NY, NX), 1.0, 6.0, ((0, 16), (2, 64)), jnp.float32)
    obs_values = gaussian(streams_of[1], (2, NY, NX), 1.0, 6.0, ((1, 64), (2, 16)), jnp.float32)
    obs_inverse_variance = jnp.clip(jnp.exp(math.log(4.0) - 2.0794415 * jax.random.uniform(streams_of[2], (2, NY, NX), jnp.float32) ** steps_of(streams_of[2], (2, NY, NX), ((1, 64), (2, 16)), -0.2, 0.2)), 0.5, 4.0)
    obs_mask = with_ends((jax.random.randint(streams_of[3], (2, NY, NX), 0, 2) < 1).astype(jnp.int32), jax.random.fold_in(streams_of[3], 1), 0, 1)
    return {"sample_collection": sample_collection, "obs_values": obs_values, "obs_inverse_variance": obs_inverse_variance, "obs_mask": obs_mask}


CADV = 0.05

def advance(dynamics_fields):
    u_field = dynamics_fields[0]
    v_field = dynamics_fields[1]

    def tendency(field):
        along_x = jnp.roll(field, -1, 1) - jnp.roll(field, 1, 1)
        along_y = jnp.roll(field, -1, 0) - jnp.roll(field, 1, 0)
        return field - CADV * (u_field * along_x + v_field * along_y)
    return jnp.stack([tendency(u_field), tendency(v_field)])

def predicted_prior(sample_fields):

    def one_member(dynamics_fields):
        for step in range(FSTEPS):
            dynamics_fields = advance(dynamics_fields)
        return dynamics_fields
    return lax.map(one_member, sample_fields)

def windows(array):
    width = array.shape[-1] - 2 * RADIUS
    count = width // PATCH
    left = array[..., :width].reshape(array.shape[:-1] + (count, PATCH))
    right = array[..., PATCH:PATCH + width].reshape(array.shape[:-1] + (count, PATCH))
    return jnp.concatenate([left, right], -1)

def taper_table():
    index = jnp.arange(2 * PATCH)
    dist = jnp.maximum(jnp.maximum(RADIUS - index, index - (RADIUS + PATCH - 1)), 0)
    far = jnp.maximum(dist[:, None], dist[None, :]).astype(jnp.float32)
    return 1.0 - far / (RADIUS + 1.0)

def analyse(dev_ext, obs_ext, mean_band):
    high = lax.Precision.HIGHEST
    region = windows(dev_ext)
    obs_region = windows(obs_ext)
    taper = taper_table()[:, None, :]
    weighted = (region.astype(jnp.float32) * (obs_region[0].astype(jnp.float32) * taper)).astype(jnp.bfloat16)
    weighted_f = weighted.astype(jnp.float32)
    gram = jnp.einsum('kvrpc,lvrpc->pkl', weighted_f, region.astype(jnp.float32), precision=high)
    projected = jnp.einsum('kvrpc,vrpc->pk', weighted_f, obs_region[1].astype(jnp.float32), precision=high)
    eye = jnp.eye(MEMBERS, dtype=jnp.float32)
    system = (MEMBERS - 1.0) * eye + gram
    scale = jnp.sqrt(lax.optimization_barrier(jnp.sum(system * system, axis=(1, 2))))[:, None, None]
    iter_y = system / scale
    iter_z = jnp.broadcast_to(eye, system.shape)
    for step in range(SCHULZ_STEPS):
        middle = 1.5 * eye - 0.5 * jnp.matmul(iter_z, iter_y, precision=high)
        iter_y = jnp.matmul(iter_y, middle, precision=high)
        iter_z = jnp.matmul(middle, iter_z, precision=high)
    root = iter_z / jnp.sqrt(scale)
    half_way = jnp.einsum('pkl,pl->pk', root, projected, precision=high)
    shift = jnp.einsum('pkl,pl->pk', root, half_way, precision=high)
    ensemble_transform = (jnp.sqrt(MEMBERS - 1.0) * root + shift[:, :, None]).astype(jnp.bfloat16)
    inner = dev_ext[:, :, RADIUS:RADIUS + PATCH, RADIUS:-RADIUS]
    inner = inner.reshape(inner.shape[:3] + (inner.shape[3] // PATCH, PATCH))
    increment = jnp.einsum('kvrpc,pkm->mvrpc', inner.astype(jnp.float32), ensemble_transform.astype(jnp.float32), precision=high)
    increment = increment.reshape(increment.shape[:3] + (-1,))
    return mean_band + increment

def wrap_columns(array):
    return jnp.concatenate([array[..., -RADIUS:], array, array[..., :RADIUS]], -1)

def reference(sample_collection, obs_values, obs_inverse_variance, obs_mask):
    leading_output = predicted_prior(sample_collection)
    mean = lax.optimization_barrier(jnp.sum(leading_output, 0)) / MEMBERS
    deviation = (leading_output - mean).astype(jnp.bfloat16)
    member_weight = (obs_mask.astype(jnp.float32) * obs_inverse_variance).astype(jnp.bfloat16)
    innovation = (obs_values - mean).astype(jnp.bfloat16)
    obs_pair = jnp.stack([member_weight, innovation])

    def band(index):
        picks = ((index * PATCH - RADIUS + jnp.arange(PATCH + 2 * RADIUS)) % NY).astype(jnp.int32)
        dev_ext = wrap_columns(jnp.take(deviation, picks, axis=2))
        obs_ext = wrap_columns(jnp.take(obs_pair, picks, axis=2))
        mean_band = lax.dynamic_slice_in_dim(mean, (index * PATCH).astype(jnp.int32), PATCH, 1)
        return analyse(dev_ext, obs_ext, mean_band)
    bands = lax.map(band, jnp.arange(NY // PATCH, dtype=jnp.int32))
    updated_estimate = jnp.transpose(bands, (1, 2, 0, 3, 4)).reshape(MEMBERS, 2, NY, NX)
    return predicted_prior(updated_estimate)
```

```python
import functools

import jax
import jax.numpy as jnp
from jax import lax
from jax.experimental import pallas as pl
from jax.experimental.pallas import tpu as pltpu
from jax.sharding import PartitionSpec as P

PATCH = 8
RADIUS = 4
FSTEPS = 4
CADV = 0.05
LANES = 128
MESH = pl.DeviceIdType.MESH
HIGHEST = lax.Precision.HIGHEST
BF16 = jnp.bfloat16
F32 = jnp.float32
I16 = jnp.int16
LIMIT = 32766.0
BOUND = 6.0


def lane_roll(value, shift):
    return pltpu.roll(value, shift % LANES, value.ndim - 1)


def advance(above, here, below):
    u_field, v_field = here

    def tendency(f):
        along_x = lane_roll(here[f], -1) - lane_roll(here[f], 1)
        along_y = below[f] - above[f]
        return here[f] - CADV * (u_field * along_x + v_field * along_y)

    return tendency(0), tendency(1)


def forecast_rows(rows):
    history = [[] for _ in range(FSTEPS)]
    done = []
    for row in rows:
        current = row
        for level in history:
            level.append(current)
            if len(level) < 3:
                current = None
                break
            current = advance(*level[-3:])
        if current is not None:
            done.append(current)
    return done


def swap_chunks(tiles):
    tiles = list(tiles)
    chunk = lax.broadcasted_iota(jnp.int32, tiles[0].shape, tiles[0].ndim - 1) // 8
    for bit in (1, 2, 4, 8):
        clear = (chunk & bit) == 0
        for i in range(16):
            if i & bit == 0:
                first, second = tiles[i], tiles[i | bit]
                tiles[i] = jnp.where(clear, first, lane_roll(second, 8 * bit))
                tiles[i | bit] = jnp.where(clear, lane_roll(first, -8 * bit), second)
    return tiles


def kernel(
    n_mem, n_rows,
    x_ref, values_ref, variance_ref, mask_ref, out_ref,
    band, band_above, band_below,
    obs, obs_above, obs_below, obs_wide, obs_left, obs_right,
    chunks, regions, unit, units, analysed, edges, own_part, above_part, below_part,
    band_send, band_recv, obs_send, obs_recv,
    region_send, region_recv, unit_send, unit_recv, own_send, own_recv, down_send, down_recv, up_send, up_recv,
):
    members = n_mem * 16
    me_mem, me_row = lax.axis_index("mem"), lax.axis_index("rows")
    above, below = lax.rem(me_row + n_rows - 1, n_rows), lax.rem(me_row + 1, n_rows)
    left, right = lax.rem(me_mem + n_mem - 1, n_mem), lax.rem(me_mem + 1, n_mem)

    def at(mem, row):
        return {"mem": mem, "rows": row}

    def remote(src, dst, send, recv, mem, row):
        return pltpu.make_async_remote_copy(
            src_ref=src, dst_ref=dst, send_sem=send, recv_sem=recv,
            device_id=at(mem, row), device_id_type=MESH,
        )

    offsets = sorted(range(1, n_mem), key=lambda d: -min(d, n_mem - d))
    partners = [lax.rem(me_mem + d, n_mem) for d in offsets]

    barrier = pltpu.get_barrier_semaphore()
    for row in (above, below):
        pl.semaphore_signal(barrier, inc=1, device_id=at(me_mem, row), device_id_type=MESH)
    for partner in partners:
        pl.semaphore_signal(barrier, inc=1, device_id=at(partner, me_row), device_id_type=MESH)

    own_rows = []
    for r in range(PATCH):
        row = tuple(lane_roll(x_ref[r, f], RADIUS) for f in range(2))
        own_rows.append(row)
        for f in range(2):
            band[r, f] = jnp.round(row[f] * (LIMIT / BOUND)).astype(I16)

    weight = (mask_ref[...].astype(F32) * variance_ref[...]).astype(BF16).astype(F32)
    planes = jnp.concatenate(
        [weight.reshape(2 * PATCH, PATCH), values_ref[...].reshape(2 * PATCH, PATCH)], 0
    )
    spread = (
        lax.broadcasted_iota(jnp.int32, (PATCH, LANES), 1) % 8
        == lax.broadcasted_iota(jnp.int32, (PATCH, LANES), 0)
    ).astype(F32)
    wide = jnp.dot(planes, spread, precision=HIGHEST, preferred_element_type=F32)
    wide = wide.reshape(4, PATCH, LANES)
    keep = (
        lax.broadcasted_iota(jnp.int32, wide.shape, 2) // 8
        == lax.broadcasted_iota(jnp.int32, wide.shape, 1) + RADIUS
    )
    wide = jnp.sum(jnp.where(keep, wide, 0.0), 1)
    obs[...] = jnp.concatenate([wide, jnp.zeros((4, LANES), F32)], 0)

    pl.semaphore_wait(barrier, n_mem + 1)

    to_below = remote(band, band_above, band_send.at[0], band_recv.at[0], me_mem, below)
    to_above = remote(band, band_below, band_send.at[1], band_recv.at[1], me_mem, above)
    to_below.start()
    to_above.start()
    obs_copies = [
        remote(obs, obs_above, obs_send.at[0], obs_recv.at[0], me_mem, below),
        remote(obs, obs_below, obs_send.at[1], obs_recv.at[1], me_mem, above),
        remote(obs_wide, obs_left, obs_send.at[2], obs_recv.at[2], right, me_row),
        remote(obs_wide, obs_right, obs_send.at[3], obs_recv.at[3], left, me_row),
    ]
    obs_copies[0].start()
    obs_copies[1].start()

    to_below.wait_recv()
    to_above.wait_recv()

    def decoded(part, r):
        return tuple(part[r, f].astype(F32) * (BOUND / LIMIT) for f in range(2))

    rows = [decoded(band_above, r) for r in range(PATCH)]
    rows += own_rows
    rows += [decoded(band_below, r) for r in range(PATCH)]
    ready = forecast_rows(rows)
    largest = jnp.abs(ready[0][0])
    for row in ready:
        for f in range(2):
            largest = jnp.maximum(largest, jnp.abs(row[f]))
    largest = jnp.max(jnp.max(largest, 0, keepdims=True), 1, keepdims=True)
    largest = jnp.maximum(largest, 1e-30)
    unit[...] = jnp.broadcast_to(largest * (1.0 / LIMIT), (1, LANES))
    grain = jnp.broadcast_to(LIMIT / largest, ready[0][0].shape)
    for f in range(2):
        tiles = swap_chunks([row[f] for row in ready])
        for j in range(n_mem):
            chunks[j, f] = jnp.round(tiles[j] * grain).astype(I16)
        chunks[n_mem, f] = chunks[0, f]

    region_copies = []
    for d, partner in zip(offsets, partners):
        copy = remote(
            chunks.at[pl.ds(partner, 2)], regions.at[me_mem],
            region_send.at[d], region_recv.at[d], partner, me_row,
        )
        copy.start()
        region_copies.append(copy)
        copy = remote(
            unit, units.at[me_mem], unit_send.at[d], unit_recv.at[d], partner, me_row
        )
        copy.start()
        region_copies.append(copy)
    regions[me_mem] = chunks[pl.ds(me_mem, 2)]
    units[me_mem] = unit[...]

    lane = lax.broadcasted_iota(jnp.int32, (8, LANES), 1)
    obs_copies[0].wait_recv()
    obs_copies[1].wait_recv()
    turned = lane_roll(jnp.where(lane >= 64, obs_above[...], obs_below[...]), 64)
    extended = jnp.where((lane >= 32) & (lane < 96), obs[...], turned)
    obs_wide[...] = extended
    obs_copies[2].start()
    obs_copies[3].start()
    obs_copies[2].wait_recv()
    obs_copies[3].wait_recv()
    lower = lane % 8 < 4
    halves = (
        jnp.where(lower, lane_roll(obs_left[...], -4), lane_roll(extended, 4)),
        jnp.where(lower, lane_roll(extended, -4), lane_roll(obs_right[...], 4)),
    )
    order = [(h, f) for h in range(2) for f in range(2)]
    weight_row = jnp.concatenate([halves[h][f : f + 1] for h, f in order], 1)
    value_row = jnp.concatenate([halves[h][2 + f : 3 + f] for h, f in order], 1)
    point = lax.broadcasted_iota(jnp.int32, (1, 4 * LANES), 1)
    region_row = point % LANES // 8
    region_col = point // (2 * LANES) * 8 + point % 8

    def distance(index):
        return jnp.maximum(jnp.maximum(RADIUS - index, index - (RADIUS + PATCH - 1)), 0)

    far = jnp.maximum(distance(region_row), distance(region_col)).astype(F32)
    factor = weight_row * (1.0 - far / (RADIUS + 1.0))

    for copy in region_copies:
        copy.wait_recv()

    every_unit = units[...]
    sample = jnp.concatenate(
        [
            (regions[:, h, f].astype(F32) * every_unit).reshape(members, LANES)
            for h, f in order
        ],
        1,
    )
    mean = jnp.sum(sample, 0, keepdims=True) / members
    deviation = (sample - mean).astype(BF16)
    innovation = (value_row - mean).astype(BF16)
    wide_deviation = deviation.astype(F32)
    weighted = (wide_deviation * factor).astype(BF16)
    stacked = jnp.concatenate(
        [deviation, jnp.broadcast_to(innovation, (16, 4 * LANES))], 0
    )
    product = lax.dot_general(
        stacked, weighted, (((1,), (1,)), ((), ())), preferred_element_type=F32
    )
    gram, projected = product[:members], product[members : members + 8]
    eye = (
        lax.broadcasted_iota(jnp.int32, (members, members), 0)
        == lax.broadcasted_iota(jnp.int32, (members, members), 1)
    ).astype(F32)
    system = (members - 1.0) * eye + gram
    square = jnp.sum(jnp.sum(system * system, 1, keepdims=True), 0, keepdims=True)
    scale = jnp.sqrt(square)

    def mul(a, b):
        return jnp.dot(a, b, precision=HIGHEST, preferred_element_type=F32)

    first_y = system / scale
    middle = 1.5 * eye - 0.5 * first_y
    iter_z = middle
    iter_y = mul(first_y, middle)
    middle = 1.5 * eye - 0.5 * mul(iter_z, iter_y)
    iter_y = mul(iter_y, middle)
    iter_z = mul(middle, iter_z)
    middle = 1.5 * eye - 0.5 * mul(iter_z, iter_y)
    iter_z = mul(middle, iter_z)
    root = iter_z / jnp.sqrt(scale)
    shift = mul(mul(projected, root), root)[0:1]
    transform = ((members - 1.0) ** 0.5 * root + shift).astype(BF16)

    inner_lane = lax.broadcasted_iota(jnp.int32, (1, LANES), 1)

    def interior(wide_value):
        fields = []
        for f in range(2):
            low = wide_value[:, f * LANES : (f + 1) * LANES]
            high = wide_value[:, (2 + f) * LANES : (3 + f) * LANES]
            fields.append(
                jnp.where(inner_lane % 8 < 4, lane_roll(low, -4), lane_roll(high, 4))
            )
        centre = (inner_lane >= 32) & (inner_lane < 96)
        return jnp.where(centre, fields[0], lane_roll(fields[1], 64))

    inner = interior(wide_deviation).astype(BF16)
    increment = jnp.dot(transform, inner, preferred_element_type=F32)
    inner_mean = interior(jnp.broadcast_to(mean, (8, 4 * LANES)))[0:1]
    analysis = (inner_mean + increment).reshape(n_mem, 16, LANES)
    analysed[...] = analysis
    edges[...] = analysis.astype(BF16)

    return_copies = []
    for d, partner in list(zip(offsets, partners)) + [(0, me_mem)]:
        pieces = [
            (edges, above_part, down_send, down_recv, below),
            (edges, below_part, up_send, up_recv, above),
        ]
        if d:
            pieces.append((analysed, own_part, own_send, own_recv, me_row))
        for source, part, send, recv, row in pieces:
            copy = remote(
                source.at[partner], part.at[me_mem], send.at[d], recv.at[d], partner, row
            )
            copy.start()
            return_copies.append(copy)
    own_part[me_mem] = analysed[me_mem]
    for copy in return_copies:
        copy.wait_recv()

    own_tiles = swap_chunks([own_part[j] for j in range(n_mem)])
    chunk = lax.broadcasted_iota(jnp.int32, (16, LANES), 1) // 8
    from_above = ((chunk >= 8) & (chunk < 12)) | (chunk < 4)
    edge_tiles = swap_chunks(
        [
            jnp.where(from_above, above_part[j].astype(F32), below_part[j].astype(F32))
            for j in range(n_mem)
        ]
    )
    rows = [(edge_tiles[8 + i], edge_tiles[i]) for i in range(4)]
    rows += [(own_tiles[4 + i], own_tiles[(12 + i) % 16]) for i in range(PATCH)]
    rows += [(edge_tiles[4 + i], edge_tiles[12 + i]) for i in range(4)]
    for r, row in enumerate(forecast_rows(rows)):
        for f in range(2):
            out_ref[r, f] = row[f]

    to_below.wait_send()
    to_above.wait_send()
    for copy in obs_copies + region_copies + return_copies:
        copy.wait_send()


def local(sample_collection, obs_values, obs_inverse_variance, obs_mask):
    n_mem, n_rows = lax.axis_size("mem"), lax.axis_size("rows")
    local_members = sample_collection.shape[0]
    vmem = pl.BlockSpec(memory_space=pltpu.VMEM)
    dma = pltpu.SemaphoreType.DMA
    band = (PATCH, 2, local_members, LANES)
    part = (n_mem, local_members, LANES)
    result = pl.pallas_call(
        functools.partial(kernel, n_mem, n_rows),
        out_shape=jax.ShapeDtypeStruct(band, F32),
        in_specs=[vmem] * 4,
        out_specs=vmem,
        scratch_shapes=[
            pltpu.VMEM(band, I16),
            pltpu.VMEM(band, I16),
            pltpu.VMEM(band, I16),
        ]
        + [pltpu.VMEM((8, LANES), F32)] * 6
        + [
            pltpu.VMEM((n_mem + 1, 2, local_members, LANES), I16),
            pltpu.VMEM((n_mem, 2, 2, local_members, LANES), I16),
            pltpu.VMEM((1, LANES), F32),
            pltpu.VMEM((n_mem, 1, LANES), F32),
            pltpu.VMEM(part, F32),
            pltpu.VMEM(part, BF16),
            pltpu.VMEM(part, F32),
            pltpu.VMEM(part, BF16),
            pltpu.VMEM(part, BF16),
        ]
        + [dma((2,)), dma((2,)), dma((4,)), dma((4,))]
        + [dma((n_mem,))] * 10,
        compiler_params=pltpu.CompilerParams(collective_id=0, has_side_effects=True),
    )(
        jnp.transpose(sample_collection, (2, 1, 0, 3)),
        obs_values,
        obs_inverse_variance,
        obs_mask,
    )
    return jnp.transpose(result, (2, 1, 0, 3))


def solution(mesh):
    return jax.shard_map(
        local,
        mesh=mesh,
        in_specs=(
            P("mem", None, "rows", None),
            P(None, "rows", "mem"),
            P(None, "rows", "mem"),
            P(None, "rows", "mem"),
        ),
        out_specs=P("mem", None, "rows", None),
        check_vma=False,
    )
```

```python
import functools

import jax
import jax.numpy as jnp
from jax import lax
from jax.experimental import pallas as pl
from jax.experimental.pallas import tpu as pltpu
from jax.sharding import PartitionSpec as P

PATCH = 8
RADIUS = 4
FSTEPS = 4
CADV = 0.05
LANES = 128
MESH = pl.DeviceIdType.MESH
HIGHEST = lax.Precision.HIGHEST
BF16 = jnp.bfloat16
F32 = jnp.float32
I16 = jnp.int16
LIMIT = 32766.0
BOUND = 6.0


def lane_roll(value, shift):
    return pltpu.roll(value, shift % LANES, value.ndim - 1)


def advance(above, here, below):
    u_field, v_field = here

    def tendency(f):
        along_x = lane_roll(here[f], -1) - lane_roll(here[f], 1)
        along_y = below[f] - above[f]
        return here[f] - CADV * (u_field * along_x + v_field * along_y)

    return tendency(0), tendency(1)


def forecast_rows(rows):
    history = [[] for _ in range(FSTEPS)]
    done = []
    for row in rows:
        current = row
        for level in history:
            level.append(current)
            if len(level) < 3:
                current = None
                break
            current = advance(*level[-3:])
        if current is not None:
            done.append(current)
    return done


def swap_chunks(tiles):
    tiles = list(tiles)
    chunk = lax.broadcasted_iota(jnp.int32, tiles[0].shape, tiles[0].ndim - 1) // 8
    for bit in (1, 2, 4, 8):
        clear = (chunk & bit) == 0
        for i in range(16):
            if i & bit == 0:
                first, second = tiles[i], tiles[i | bit]
                tiles[i] = jnp.where(clear, first, lane_roll(second, 8 * bit))
                tiles[i | bit] = jnp.where(clear, lane_roll(first, -8 * bit), second)
    return tiles


def kernel(
    n_mem, n_rows,
    x_ref, values_ref, variance_ref, mask_ref, out_ref,
    x_local, values, variance, mask,
    band, band_above, band_below,
    obs, obs_above, obs_below, obs_wide, obs_left, obs_right,
    chunks, regions, unit, units, analysed, edges, own_part, above_part, below_part,
    rows_ready, mem_ready, load_sem, band_send, band_recv, obs_send, obs_recv,
    region_send, region_recv, unit_send, unit_recv, own_send, own_recv, down_send, down_recv, up_send, up_recv,
):
    members = n_mem * 16
    me_mem, me_row = lax.axis_index("mem"), lax.axis_index("rows")
    above, below = lax.rem(me_row + n_rows - 1, n_rows), lax.rem(me_row + 1, n_rows)
    left, right = lax.rem(me_mem + n_mem - 1, n_mem), lax.rem(me_mem + 1, n_mem)

    def at(mem, row):
        return {"mem": mem, "rows": row}

    def remote(src, dst, send, recv, mem, row):
        return pltpu.make_async_remote_copy(
            src_ref=src, dst_ref=dst, send_sem=send, recv_sem=recv,
            device_id=at(mem, row), device_id_type=MESH,
        )

    offsets = sorted(range(1, n_mem), key=lambda d: -min(d, n_mem - d))
    partners = [lax.rem(me_mem + d, n_mem) for d in offsets]

    barrier = pltpu.get_barrier_semaphore()
    even = lax.rem(me_row, 2) == 0
    above_two = lax.rem(me_row + n_rows - 2, n_rows)
    odd_row = me_row + 1 - lax.rem(me_row, 2)

    def greet(semaphore, mem, row):
        pl.semaphore_signal(semaphore, inc=1, device_id=at(mem, row), device_id_type=MESH)

    @pl.when(even)
    def _():
        greet(barrier, me_mem, above_two)

    @pl.when(jnp.logical_not(even))
    def _():
        greet(barrier, me_mem, below)
        greet(barrier, me_mem, above)

    for partner in partners:
        greet(barrier, partner, odd_row)

    loads = [
        pltpu.make_async_copy(source, target, load_sem.at[i])
        for i, (source, target) in enumerate(
            [
                (x_ref, x_local),
                (values_ref, values),
                (variance_ref, variance),
                (mask_ref, mask),
            ]
        )
    ]
    for load in loads:
        load.start()
    loads[0].wait()

    def rows_of(ref, r, f):
        return ref.at[pl.ds(f * PATCH + r, 16, stride=2 * PATCH), :]

    own_rows = []
    for r in range(PATCH):
        row = tuple(lane_roll(rows_of(x_local, r, f)[...], RADIUS) for f in range(2))
        own_rows.append(row)
        for f in range(2):
            band[r, f] = jnp.round(row[f] * (LIMIT / BOUND)).astype(I16)

    @pl.when(even)
    def _():
        pl.semaphore_wait(barrier, 3)
        greet(rows_ready, me_mem, below)

    @pl.when(jnp.logical_not(even))
    def _():
        pl.semaphore_wait(rows_ready, 1)

    to_below = remote(band, band_above, band_send.at[0], band_recv.at[0], me_mem, below)
    to_above = remote(band, band_below, band_send.at[1], band_recv.at[1], me_mem, above)
    to_below.start()
    to_above.start()

    for load in loads[1:]:
        load.wait()
    weight = (mask[...].astype(F32) * variance[...]).astype(BF16).astype(F32)
    planes = jnp.concatenate(
        [weight.reshape(2 * PATCH, PATCH), values[...].reshape(2 * PATCH, PATCH)], 0
    )
    spread = (
        lax.broadcasted_iota(jnp.int32, (PATCH, LANES), 1) % 8
        == lax.broadcasted_iota(jnp.int32, (PATCH, LANES), 0)
    ).astype(F32)
    wide = jnp.dot(planes, spread, precision=HIGHEST, preferred_element_type=F32)
    wide = wide.reshape(4, PATCH, LANES)
    keep = (
        lax.broadcasted_iota(jnp.int32, wide.shape, 2) // 8
        == lax.broadcasted_iota(jnp.int32, wide.shape, 1) + RADIUS
    )
    wide = jnp.sum(jnp.where(keep, wide, 0.0), 1)
    obs[...] = jnp.concatenate([wide, jnp.zeros((4, LANES), F32)], 0)

    obs_copies = [
        remote(obs, obs_above, obs_send.at[0], obs_recv.at[0], me_mem, below),
        remote(obs, obs_below, obs_send.at[1], obs_recv.at[1], me_mem, above),
        remote(obs_wide, obs_left, obs_send.at[2], obs_recv.at[2], right, me_row),
        remote(obs_wide, obs_right, obs_send.at[3], obs_recv.at[3], left, me_row),
    ]
    obs_copies[0].start()
    obs_copies[1].start()

    to_below.wait_recv()
    to_above.wait_recv()

    def decoded(part, r):
        return tuple(part[r, f].astype(F32) * (BOUND / LIMIT) for f in range(2))

    rows = [decoded(band_above, r) for r in range(PATCH)]
    rows += own_rows
    rows += [decoded(band_below, r) for r in range(PATCH)]
    ready = forecast_rows(rows)
    largest = jnp.abs(ready[0][0])
    for row in ready:
        for f in range(2):
            largest = jnp.maximum(largest, jnp.abs(row[f]))
    largest = jnp.max(jnp.max(largest, 0, keepdims=True), 1, keepdims=True)
    largest = jnp.maximum(largest, 1e-30)
    unit[...] = jnp.broadcast_to(largest * (1.0 / LIMIT), (1, LANES))
    grain = jnp.broadcast_to(LIMIT / largest, ready[0][0].shape)
    for f in range(2):
        tiles = swap_chunks([row[f] for row in ready])
        for j in range(n_mem):
            chunks[j, f] = jnp.round(tiles[j] * grain).astype(I16)
        chunks[n_mem, f] = chunks[0, f]

    @pl.when(jnp.logical_not(even))
    def _():
        pl.semaphore_wait(barrier, 2 * (n_mem - 1))
        greet(mem_ready, me_mem, above)

    @pl.when(even)
    def _():
        pl.semaphore_wait(mem_ready, 1)

    region_copies = []
    for d, partner in zip(offsets, partners):
        copy = remote(
            chunks.at[pl.ds(partner, 2)], regions.at[me_mem],
            region_send.at[d], region_recv.at[d], partner, me_row,
        )
        copy.start()
        region_copies.append(copy)
        copy = remote(
            unit, units.at[me_mem], unit_send.at[d], unit_recv.at[d], partner, me_row
        )
        copy.start()
        region_copies.append(copy)
    regions[me_mem] = chunks[pl.ds(me_mem, 2)]
    units[me_mem] = unit[...]

    lane = lax.broadcasted_iota(jnp.int32, (8, LANES), 1)
    obs_copies[0].wait_recv()
    obs_copies[1].wait_recv()
    turned = lane_roll(jnp.where(lane >= 64, obs_above[...], obs_below[...]), 64)
    extended = jnp.where((lane >= 32) & (lane < 96), obs[...], turned)
    obs_wide[...] = extended
    obs_copies[2].start()
    obs_copies[3].start()
    obs_copies[2].wait_recv()
    obs_copies[3].wait_recv()
    lower = lane % 8 < 4
    halves = (
        jnp.where(lower, lane_roll(obs_left[...], -4), lane_roll(extended, 4)),
        jnp.where(lower, lane_roll(extended, -4), lane_roll(obs_right[...], 4)),
    )
    order = [(h, f) for h in range(2) for f in range(2)]
    weight_row = jnp.concatenate([halves[h][f : f + 1] for h, f in order], 1)
    value_row = jnp.concatenate([halves[h][2 + f : 3 + f] for h, f in order], 1)
    point = lax.broadcasted_iota(jnp.int32, (1, 4 * LANES), 1)
    region_row = point % LANES // 8
    region_col = point // (2 * LANES) * 8 + point % 8

    def distance(index):
        return jnp.maximum(jnp.maximum(RADIUS - index, index - (RADIUS + PATCH - 1)), 0)

    far = jnp.maximum(distance(region_row), distance(region_col)).astype(F32)
    factor = weight_row * (1.0 - far / (RADIUS + 1.0))

    for copy in region_copies:
        copy.wait_recv()

    every_unit = units[...]
    sample = jnp.concatenate(
        [
            (regions[:, h, f].astype(F32) * every_unit).reshape(members, LANES)
            for h, f in order
        ],
        1,
    )
    mean = jnp.sum(sample, 0, keepdims=True) / members
    deviation = (sample - mean).astype(BF16)
    innovation = (value_row - mean).astype(BF16)
    wide_deviation = deviation.astype(F32)
    weighted = (wide_deviation * factor).astype(BF16)
    stacked = jnp.concatenate(
        [deviation, jnp.broadcast_to(innovation, (16, 4 * LANES))], 0
    )
    product = lax.dot_general(
        stacked, weighted, (((1,), (1,)), ((), ())), preferred_element_type=F32
    )
    gram, projected = product[:members], product[members : members + 8]
    eye = (
        lax.broadcasted_iota(jnp.int32, (members, members), 0)
        == lax.broadcasted_iota(jnp.int32, (members, members), 1)
    ).astype(F32)
    system = (members - 1.0) * eye + gram
    square = jnp.sum(jnp.sum(system * system, 1, keepdims=True), 0, keepdims=True)
    scale = jnp.sqrt(square)

    def mul(a, b):
        return jnp.dot(a, b, precision=lax.Precision.HIGH, preferred_element_type=F32)

    first_y = system / scale
    middle = 1.5 * eye - 0.5 * first_y
    iter_z = middle
    iter_y = mul(first_y, middle)
    middle = 1.5 * eye - 0.5 * mul(iter_z, iter_y)
    iter_y = mul(iter_y, middle)
    iter_z = mul(middle, iter_z)
    middle = 1.5 * eye - 0.5 * mul(iter_z, iter_y)
    iter_z = mul(middle, iter_z)
    root = iter_z / jnp.sqrt(scale)
    shift = mul(mul(projected, root), root)[0:1]
    transform = ((members - 1.0) ** 0.5 * root + shift).astype(BF16)

    inner_lane = lax.broadcasted_iota(jnp.int32, (1, LANES), 1)

    def interior(wide_value):
        fields = []
        for f in range(2):
            low = wide_value[:, f * LANES : (f + 1) * LANES]
            high = wide_value[:, (2 + f) * LANES : (3 + f) * LANES]
            fields.append(
                jnp.where(inner_lane % 8 < 4, lane_roll(low, -4), lane_roll(high, 4))
            )
        centre = (inner_lane >= 32) & (inner_lane < 96)
        return jnp.where(centre, fields[0], lane_roll(fields[1], 64))

    inner = interior(wide_deviation).astype(BF16)
    increment = jnp.dot(transform, inner, preferred_element_type=F32)
    inner_mean = interior(jnp.broadcast_to(mean, (8, 4 * LANES)))[0:1]
    analysis = (inner_mean + increment).reshape(n_mem, 16, LANES)
    analysed[...] = analysis
    edges[...] = analysis.astype(BF16)

    return_copies = []
    for d, partner in list(zip(offsets, partners)) + [(0, me_mem)]:
        pieces = [
            (edges, above_part, down_send, down_recv, below),
            (edges, below_part, up_send, up_recv, above),
        ]
        if d:
            pieces.append((analysed, own_part, own_send, own_recv, me_row))
        for source, part, send, recv, row in pieces:
            copy = remote(
                source.at[partner], part.at[me_mem], send.at[d], recv.at[d], partner, row
            )
            copy.start()
            return_copies.append(copy)
    own_part[me_mem] = analysed[me_mem]
    for copy in return_copies:
        copy.wait_recv()

    own_tiles = swap_chunks([own_part[j] for j in range(n_mem)])
    chunk = lax.broadcasted_iota(jnp.int32, (16, LANES), 1) // 8
    from_above = ((chunk >= 8) & (chunk < 12)) | (chunk < 4)
    edge_tiles = swap_chunks(
        [
            jnp.where(from_above, above_part[j].astype(F32), below_part[j].astype(F32))
            for j in range(n_mem)
        ]
    )
    rows = [(edge_tiles[8 + i], edge_tiles[i]) for i in range(4)]
    rows += [(own_tiles[4 + i], own_tiles[(12 + i) % 16]) for i in range(PATCH)]
    rows += [(edge_tiles[4 + i], edge_tiles[12 + i]) for i in range(4)]
    for r, row in enumerate(forecast_rows(rows)):
        for f in range(2):
            rows_of(out_ref, r, f)[...] = row[f]

    to_below.wait_send()
    to_above.wait_send()
    for copy in obs_copies + region_copies + return_copies:
        copy.wait_send()


def local(sample_collection, obs_values, obs_inverse_variance, obs_mask):
    n_mem, n_rows = lax.axis_size("mem"), lax.axis_size("rows")
    local_members = sample_collection.shape[0]
    dma = pltpu.SemaphoreType.DMA
    band = (PATCH, 2, local_members, LANES)
    flat = (local_members * 2 * PATCH, LANES)
    part = (n_mem, local_members, LANES)
    result = pl.pallas_call(
        functools.partial(kernel, n_mem, n_rows),
        out_shape=pltpu.VMEM(flat, F32),
        in_specs=[pl.BlockSpec(memory_space=pl.ANY)] * 4,
        out_specs=pl.BlockSpec(memory_space=pltpu.VMEM),
        scratch_shapes=[
            pltpu.VMEM(flat, F32),
            pltpu.VMEM(obs_values.shape, F32),
            pltpu.VMEM(obs_values.shape, F32),
            pltpu.VMEM(obs_values.shape, jnp.int32),
            pltpu.VMEM(band, I16),
            pltpu.VMEM(band, I16),
            pltpu.VMEM(band, I16),
        ]
        + [pltpu.VMEM((8, LANES), F32)] * 6
        + [
            pltpu.VMEM((n_mem + 1, 2, local_members, LANES), I16),
            pltpu.VMEM((n_mem, 2, 2, local_members, LANES), I16),
            pltpu.VMEM((1, LANES), F32),
            pltpu.VMEM((n_mem, 1, LANES), F32),
            pltpu.VMEM(part, F32),
            pltpu.VMEM(part, BF16),
            pltpu.VMEM(part, F32),
            pltpu.VMEM(part, BF16),
            pltpu.VMEM(part, BF16),
        ]
        + [pltpu.SemaphoreType.REGULAR, pltpu.SemaphoreType.REGULAR]
        + [dma((4,)), dma((2,)), dma((2,)), dma((4,)), dma((4,))]
        + [dma((n_mem,))] * 10,
        compiler_params=pltpu.CompilerParams(collective_id=0, has_side_effects=True),
    )(
        sample_collection.reshape(flat),
        obs_values,
        obs_inverse_variance,
        obs_mask,
    )
    return result.reshape(sample_collection.shape)


def solution(mesh):
    return jax.shard_map(
        local,
        mesh=mesh,
        in_specs=(
            P("mem", None, "rows", None),
            P(None, "rows", "mem"),
            P(None, "rows", "mem"),
            P(None, "rows", "mem"),
        ),
        out_specs=P("mem", None, "rows", None),
        check_vma=False,
    )
```

```python
import functools

import jax
import jax.numpy as jnp
from jax import lax
from jax.experimental import pallas as pl
from jax.experimental.pallas import tpu as pltpu
from jax.sharding import PartitionSpec as P

PATCH = 8
RADIUS = 4
FSTEPS = 4
SCHULZ_STEPS = 3
CADV = 0.05
LANES = 128
MESH = pl.DeviceIdType.MESH
HIGHEST = lax.Precision.HIGHEST
BF16 = jnp.bfloat16
F32 = jnp.float32
LIMIT = 32766.0
BOUND = 6.0


def lane_roll(value, shift):
    return pltpu.roll(value, shift % LANES, value.ndim - 1)


def advance(above, here, below):
    u_field, v_field = here

    def tendency(f):
        along_x = lane_roll(here[f], -1) - lane_roll(here[f], 1)
        along_y = below[f] - above[f]
        return here[f] - CADV * (u_field * along_x + v_field * along_y)

    return tendency(0), tendency(1)


def forecast_rows(rows):
    history = [[] for _ in range(FSTEPS)]
    done = []
    for row in rows:
        current = row
        for level in history:
            level.append(current)
            if len(level) < 3:
                current = None
                break
            current = advance(*level[-3:])
        if current is not None:
            done.append(current)
    return done


def swap_chunks(tiles):
    tiles = list(tiles)
    chunk = lax.broadcasted_iota(jnp.int32, tiles[0].shape, tiles[0].ndim - 1) // 8
    for bit in (1, 2, 4, 8):
        clear = (chunk & bit) == 0
        for i in range(16):
            if i & bit == 0:
                first, second = tiles[i], tiles[i | bit]
                tiles[i] = jnp.where(clear, first, lane_roll(second, 8 * bit))
                tiles[i | bit] = jnp.where(clear, lane_roll(first, -8 * bit), second)
    return tiles


def top_lanes(shape):
    chunk = lax.broadcasted_iota(jnp.int32, shape, len(shape) - 1) // 8
    return (chunk & 4) != 0


def pair_codes(low, high):
    low, high = (jnp.round(v).astype(jnp.int32) for v in (low, high))
    return (high << 16) | (low & 0xFFFF)


def codes_of(word):
    return ((word << 16) >> 16).astype(F32), (word >> 16).astype(F32)


def unit_of(values):
    largest = functools.reduce(jnp.maximum, [jnp.abs(v) for v in values])
    largest = jnp.max(jnp.max(largest, 0, keepdims=True), 1, keepdims=True)
    largest = jnp.maximum(largest, 1e-30)
    return jnp.broadcast_to(largest * (1.0 / LIMIT), (1, LANES)), LIMIT / largest


def kernel(
    n_mem, n_rows,
    x_ref, values_ref, variance_ref, mask_ref, out_ref,
    x_local, values, variance, mask,
    band, band_above, band_below,
    obs, obs_above, obs_below, obs_wide, obs_left, obs_right,
    chunks, regions, unit, units, back_unit, back_units, analysed, edges_up, edges_down, own_part, above_part, below_part,
    token, load_sem, band_send, band_recv, obs_send, obs_recv,
    region_send, region_recv, unit_send, unit_recv, own_send, own_recv, back_send, back_recv, down_send, down_recv, up_send, up_recv,
):
    members = n_mem * 16
    me_mem, me_row = lax.axis_index("mem"), lax.axis_index("rows")
    above, below = lax.rem(me_row + n_rows - 1, n_rows), lax.rem(me_row + 1, n_rows)
    left, right = lax.rem(me_mem + n_mem - 1, n_mem), lax.rem(me_mem + 1, n_mem)

    def at(mem, row):
        return {"mem": mem, "rows": row}

    def remote(src, dst, send, recv, mem, row):
        return pltpu.make_async_remote_copy(
            src_ref=src, dst_ref=dst, send_sem=send, recv_sem=recv,
            device_id=at(mem, row), device_id_type=MESH,
        )

    offsets = sorted(range(1, n_mem), key=lambda d: -min(d, n_mem - d))
    partners = [lax.rem(me_mem + d, n_mem) for d in offsets]

    barrier = pltpu.get_barrier_semaphore()

    def ring(mem, step):
        return lax.rem(mem + step + n_mem, n_mem)

    def greet(semaphore, mem, row):
        pl.semaphore_signal(semaphore, inc=1, device_id=at(mem, row), device_id_type=MESH)

    pair = me_mem + 1 - 2 * lax.rem(me_mem, 2)
    near = [pair] + [ring(mem, step) for mem in (me_mem, pair) for step in (4, -4, 2, -2)]
    for row in (above, below):
        greet(barrier, me_mem, row)
    for mem in near:
        greet(barrier, mem, me_row)

    loads = [
        pltpu.make_async_copy(source, target, load_sem.at[i])
        for i, (source, target) in enumerate(
            [
                (x_ref, x_local),
                (values_ref, values),
                (variance_ref, variance),
                (mask_ref, mask),
            ]
        )
    ]
    for load in loads:
        load.start()
    loads[0].wait()

    def rows_of(ref, r, f):
        return ref.at[pl.ds(f * PATCH + r, 16, stride=2 * PATCH), :]

    own_rows = []
    for r in range(PATCH):
        row = tuple(lane_roll(rows_of(x_local, r, f)[...], RADIUS) for f in range(2))
        own_rows.append(row)
        band[r] = pair_codes(*(value * (LIMIT / BOUND) for value in row))

    pl.semaphore_wait(barrier, 2 + len(near))

    to_below = remote(band, band_above, band_send.at[0], band_recv.at[0], me_mem, below)
    to_above = remote(band, band_below, band_send.at[1], band_recv.at[1], me_mem, above)
    to_below.start()
    to_above.start()
    for step in (4, -4):
        greet(token, ring(me_mem, step), me_row)

    for load in loads[1:]:
        load.wait()
    weight = (mask[...].astype(F32) * variance[...]).astype(BF16).astype(F32)
    planes = jnp.concatenate(
        [weight.reshape(2 * PATCH, PATCH), values[...].reshape(2 * PATCH, PATCH)], 0
    )
    spread = (
        lax.broadcasted_iota(jnp.int32, (PATCH, LANES), 1) % 8
        == lax.broadcasted_iota(jnp.int32, (PATCH, LANES), 0)
    ).astype(F32)
    wide = jnp.dot(planes, spread, precision=HIGHEST, preferred_element_type=F32)
    wide = wide.reshape(4, PATCH, LANES)
    keep = (
        lax.broadcasted_iota(jnp.int32, wide.shape, 2) // 8
        == lax.broadcasted_iota(jnp.int32, wide.shape, 1) + RADIUS
    )
    wide = jnp.sum(jnp.where(keep, wide, 0.0), 1)
    obs[...] = jnp.concatenate([wide, jnp.zeros((4, LANES), F32)], 0)

    obs_copies = [
        remote(obs, obs_above, obs_send.at[0], obs_recv.at[0], me_mem, below),
        remote(obs, obs_below, obs_send.at[1], obs_recv.at[1], me_mem, above),
        remote(obs_wide, obs_left, obs_send.at[2], obs_recv.at[2], right, me_row),
        remote(obs_wide, obs_right, obs_send.at[3], obs_recv.at[3], left, me_row),
    ]
    obs_copies[0].start()
    obs_copies[1].start()

    to_below.wait_recv()
    to_above.wait_recv()

    def rows_in(part, half):
        words = [part[r, 8 * half : 8 * half + 8] for r in range(PATCH)]
        return [tuple(v * (BOUND / LIMIT) for v in codes_of(word)) for word in words]

    for half in range(2):
        rows = rows_in(band_above, half)
        rows += [tuple(v[8 * half : 8 * half + 8] for v in row) for row in own_rows]
        rows += rows_in(band_below, half)
        ready = forecast_rows(rows)
        unit[half], grain = unit_of([v for row in ready for v in row])
        grain = jnp.broadcast_to(grain, (8, LANES))
        tiles = swap_chunks([pair_codes(*(v * grain for v in row)) for row in ready])
        for j in range(n_mem):
            chunks[half, j] = tiles[j]
        chunks[half, n_mem] = tiles[0]

        if half == 0:
            pl.semaphore_wait(token, 2)

        for partner in partners:
            remote(
                chunks.at[half, pl.ds(partner, 2)], regions.at[me_mem, half],
                region_send, region_recv, partner, me_row,
            ).start()
    for partner in partners:
        remote(unit, units.at[me_mem], unit_send, unit_recv, partner, me_row).start()
    for half in range(2):
        regions[me_mem, half] = chunks[half, pl.ds(me_mem, 2)]
    units[me_mem] = unit[...]

    lane = lax.broadcasted_iota(jnp.int32, (8, LANES), 1)
    obs_copies[0].wait_recv()
    obs_copies[1].wait_recv()
    turned = lane_roll(jnp.where(lane >= 64, obs_above[...], obs_below[...]), 64)
    extended = jnp.where((lane >= 32) & (lane < 96), obs[...], turned)
    obs_wide[...] = extended
    obs_copies[2].start()
    obs_copies[3].start()
    obs_copies[2].wait_recv()
    obs_copies[3].wait_recv()
    lower = lane % 8 < 4
    halves = (
        jnp.where(lower, lane_roll(obs_left[...], -4), lane_roll(extended, 4)),
        jnp.where(lower, lane_roll(extended, -4), lane_roll(obs_right[...], 4)),
    )
    order = [(h, f) for h in range(2) for f in range(2)]
    weight_row = jnp.concatenate([halves[h][f : f + 1] for h, f in order], 1)
    value_row = jnp.concatenate([halves[h][2 + f : 3 + f] for h, f in order], 1)
    point = lax.broadcasted_iota(jnp.int32, (1, 4 * LANES), 1)
    region_row = point % LANES // 8
    region_col = point // (2 * LANES) * 8 + point % 8

    def distance(index):
        return jnp.maximum(jnp.maximum(RADIUS - index, index - (RADIUS + PATCH - 1)), 0)

    far = jnp.maximum(distance(region_row), distance(region_col)).astype(F32)
    factor = weight_row * (1.0 - far / (RADIUS + 1.0))

    column = lax.broadcasted_iota(jnp.int32, (4 * LANES, 2 * LANES), 1)
    lane = column % LANES
    turn = jnp.where((lane & 32) != 0, 32, LANES - 32)
    lane = jnp.where(column < LANES, lane, (lane + turn) % LANES)
    field = 1 - ((lane >= 32) & (lane < 96)).astype(jnp.int32)
    grid_row = (lane // 8 + 8 * field) % 16
    grid_col = lane % 8 + RADIUS
    source = (grid_col // 8 * 2 + field) * LANES + grid_row * 8 + grid_col % 8
    select = (lax.broadcasted_iota(jnp.int32, lane.shape, 0) == source).astype(BF16)

    others = n_mem - 1

    def whole(buffer, count, send, recv):
        part = buffer.at[pl.ds(0, count)]
        return remote(part, part, send, recv, right, me_row)

    region_all = whole(regions, others, region_send, region_recv)
    unit_all = whole(units, others, unit_send, unit_recv)
    region_all.wait_recv()
    unit_all.wait_recv()

    every_unit = units[...]
    fields = []
    for h in range(2):
        for code in codes_of(regions[:, :, h]):
            fields.append((code * every_unit).reshape(members, LANES))
    sample = jnp.concatenate(fields, 1)
    mean = jnp.sum(sample, 0, keepdims=True) / members
    deviation = (sample - mean).astype(BF16)
    innovation = (value_row - mean).astype(BF16)
    weighted = (deviation.astype(F32) * factor).astype(BF16)
    inner = jnp.dot(deviation, select, preferred_element_type=F32).astype(BF16)
    stacked = jnp.concatenate(
        [deviation, jnp.broadcast_to(innovation, (16, 4 * LANES))], 0
    )
    product = lax.dot_general(
        stacked, weighted, (((1,), (1,)), ((), ())), preferred_element_type=F32
    )
    gram, projected = product[:members], product[members : members + 8]
    eye = (
        lax.broadcasted_iota(jnp.int32, (members, members), 0)
        == lax.broadcasted_iota(jnp.int32, (members, members), 1)
    ).astype(F32)
    system = (members - 1.0) * eye + gram
    square = jnp.sum(jnp.sum(system * system, 1, keepdims=True), 0, keepdims=True)
    scale = jnp.sqrt(square)

    def mul(a, b):
        return jnp.dot(a.astype(BF16), b.astype(BF16), preferred_element_type=F32)

    y = system * (1.0 / scale)
    y2 = mul(y, y)
    y3 = mul(y, y2)
    y4 = mul(y2, y2)
    y5 = mul(y2, y3)
    zy1 = 2.25 * y - 1.5 * y2 + 0.25 * y3
    zyy1 = 2.25 * y2 - 1.5 * y3 + 0.25 * y4
    zyyy1 = 2.25 * y3 - 1.5 * y4 + 0.25 * y5
    e2 = 0.25 * zyy1 - 0.75 * (y + zy1)
    iter_y = 2.25 * y - 0.75 * (y2 + zyy1) + 0.25 * zyyy1
    zy2 = 2.25 * iter_y + mul(e2, iter_y)
    e3 = 1.5 * e2 - 1.125 * zy2 - 0.5 * mul(zy2, e2)
    lead = (1.5**SCHULZ_STEPS) * eye
    shrink = lax.rsqrt(scale)
    root = (lead + e3) * shrink
    half_way = (1.5**SCHULZ_STEPS) * projected + mul(projected, e3)
    shift = ((1.5**SCHULZ_STEPS) * half_way + mul(half_way, e3)) / scale
    shift = shift[0:1]
    transform = ((members - 1.0) ** 0.5 * root + shift).astype(BF16)

    inner_lane = lax.broadcasted_iota(jnp.int32, (1, LANES), 1)

    def interior(wide_value):
        fields = []
        for f in range(2):
            low = wide_value[:, f * LANES : (f + 1) * LANES]
            high = wide_value[:, (2 + f) * LANES : (3 + f) * LANES]
            fields.append(
                jnp.where(inner_lane % 8 < 4, lane_roll(low, -4), lane_roll(high, 4))
            )
        centre = (inner_lane >= 32) & (inner_lane < 96)
        return jnp.where(centre, fields[0], lane_roll(fields[1], 64))

    increment = jnp.dot(transform, inner, preferred_element_type=F32)
    inner_mean = interior(jnp.broadcast_to(mean, (8, 4 * LANES)))[0:1]
    top = top_lanes((8, LANES))
    mean_rows = jnp.broadcast_to(inner_mean, (8, LANES))
    turned_mean = jnp.where(top, lane_roll(mean_rows, -32), lane_roll(mean_rows, 32))[0:1]
    analysis = inner_mean + increment[:, :LANES]
    turned = turned_mean + increment[:, LANES:]
    parts = (n_mem, 2, 8, LANES)
    first, second = analysis.reshape(parts)[:, 0], turned.reshape(parts)[:, 1]
    top = top_lanes(first.shape)
    edges_up[...] = jnp.where(top, first, second).astype(BF16)
    edges_down[...] = jnp.where(top, second, first).astype(BF16)

    for partner in partners + [me_mem]:
        remote(
            edges_down.at[partner], above_part.at[me_mem], down_send, down_recv, partner, below
        ).start()
        remote(
            edges_up.at[partner], below_part.at[me_mem], up_send, up_recv, partner, above
        ).start()
    back_unit[...], grain = unit_of([analysis])
    scaled = (analysis * grain).reshape(parts)
    analysed[...] = pair_codes(scaled[:, 0], scaled[:, 1])
    for partner in partners:
        remote(
            analysed.at[partner], own_part.at[me_mem], own_send, own_recv, partner, me_row
        ).start()
    for partner in partners:
        remote(
            back_unit, back_units.at[me_mem], back_send, back_recv, partner, me_row
        ).start()
    own_part[me_mem] = analysed[me_mem]
    back_units[me_mem] = back_unit[...]
    to_below.wait_send()
    to_above.wait_send()
    for copy in obs_copies:
        copy.wait_send()
    region_all.wait_send()
    unit_all.wait_send()
    down_all = whole(above_part, n_mem, down_send, down_recv)
    up_all = whole(below_part, n_mem, up_send, up_recv)
    own_all = whole(own_part, others, own_send, own_recv)
    back_all = whole(back_units, others, back_send, back_recv)
    own_all.wait_recv()
    back_all.wait_recv()
    source = lax.broadcasted_iota(jnp.int32, (n_mem, LANES), 0)
    lane = lax.broadcasted_iota(jnp.int32, (n_mem, LANES), 1)
    unit_row = jnp.sum(
        jnp.where(lane // 8 == source, back_units[...].reshape(n_mem, LANES), 0.0),
        0,
        keepdims=True,
    )
    own_tiles = [
        jnp.concatenate([v * unit_row for v in codes_of(tile)], 0)
        for tile in swap_chunks([own_part[j] for j in range(n_mem)])
    ]
    down_all.wait_recv()
    up_all.wait_recv()
    edge_tiles = swap_chunks(
        [
            jnp.concatenate([below_part[j].astype(F32), above_part[j].astype(F32)], 0)
            for j in range(n_mem)
        ]
    )

    def edge_row(part, first, second):
        pick = slice(8 * part, 8 * part + 8)
        return jnp.concatenate([edge_tiles[first][pick], edge_tiles[second][pick]], 0)

    rows = [(edge_row(1, 8 + i, 4 + i), edge_row(1, i, 12 + i)) for i in range(4)]
    rows += [(own_tiles[4 + i], own_tiles[(12 + i) % 16]) for i in range(PATCH)]
    rows += [(edge_row(0, 4 + i, 8 + i), edge_row(0, 12 + i, i)) for i in range(4)]
    for r, row in enumerate(forecast_rows(rows)):
        for f in range(2):
            rows_of(out_ref, r, f)[...] = row[f]

    for copies in (own_all, back_all, down_all, up_all):
        copies.wait_send()


def local(sample_collection, obs_values, obs_inverse_variance, obs_mask):
    n_mem, n_rows = lax.axis_size("mem"), lax.axis_size("rows")
    local_members = sample_collection.shape[0]
    dma = pltpu.SemaphoreType.DMA
    band = (PATCH, local_members, LANES)
    flat = (local_members * 2 * PATCH, LANES)
    part = (n_mem, local_members // 2, LANES)
    result = pl.pallas_call(
        functools.partial(kernel, n_mem, n_rows),
        out_shape=pltpu.VMEM(flat, F32),
        in_specs=[pl.BlockSpec(memory_space=pl.ANY)] * 4,
        out_specs=pl.BlockSpec(memory_space=pltpu.VMEM),
        scratch_shapes=[
            pltpu.VMEM(flat, F32),
            pltpu.VMEM(obs_values.shape, F32),
            pltpu.VMEM(obs_values.shape, F32),
            pltpu.VMEM(obs_values.shape, jnp.int32),
        ]
        + [pltpu.VMEM(band, jnp.int32)] * 3
        + [pltpu.VMEM((8, LANES), F32)] * 6
        + [
            pltpu.VMEM((2, n_mem + 1, 8, LANES), jnp.int32),
            pltpu.VMEM((n_mem, 2, 2, 8, LANES), jnp.int32),
            pltpu.VMEM((2, 1, LANES), F32),
            pltpu.VMEM((n_mem, 2, 1, LANES), F32),
            pltpu.VMEM((1, LANES), F32),
            pltpu.VMEM((n_mem, 1, LANES), F32),
            pltpu.VMEM(part, jnp.int32),
            pltpu.VMEM(part, BF16),
            pltpu.VMEM(part, BF16),
            pltpu.VMEM(part, jnp.int32),
            pltpu.VMEM(part, BF16),
            pltpu.VMEM(part, BF16),
        ]
        + [pltpu.SemaphoreType.REGULAR]
        + [dma((4,)), dma((2,)), dma((2,)), dma((4,)), dma((4,))]
        + [dma(())] * 12,
        compiler_params=pltpu.CompilerParams(collective_id=0, has_side_effects=True),
    )(
        sample_collection.reshape(flat),
        obs_values,
        obs_inverse_variance,
        obs_mask,
    )
    return result.reshape(sample_collection.shape)


def solution(mesh):
    return jax.shard_map(
        local,
        mesh=mesh,
        in_specs=(
            P("mem", None, "rows", None),
            P(None, "rows", "mem"),
            P(None, "rows", "mem"),
            P(None, "rows", "mem"),
        ),
        out_specs=P("mem", None, "rows", None),
        check_vma=False,
    )
```

```python
import functools

import jax
import jax.numpy as jnp
from jax import lax
from jax.experimental import pallas as pl
from jax.experimental.pallas import tpu as pltpu
from jax.sharding import PartitionSpec as P

PATCH = 8
RADIUS = 4
FSTEPS = 4
SCHULZ_STEPS = 3
CADV = 0.05
LANES = 128
MESH = pl.DeviceIdType.MESH
HIGHEST = lax.Precision.HIGHEST
BF16 = jnp.bfloat16
F32 = jnp.float32
LIMIT = 32766.0
BOUND = 6.0


def lane_roll(value, shift):
    return pltpu.roll(value, shift % LANES, value.ndim - 1)


def advance(above, here, below):
    u_field, v_field = here

    def tendency(f):
        along_x = lane_roll(here[f], -1) - lane_roll(here[f], 1)
        along_y = below[f] - above[f]
        return here[f] - CADV * (u_field * along_x + v_field * along_y)

    return tendency(0), tendency(1)


def forecast_rows(rows):
    history = [[] for _ in range(FSTEPS)]
    done = []
    for row in rows:
        current = row
        for level in history:
            level.append(current)
            if len(level) < 3:
                current = None
                break
            current = advance(*level[-3:])
        if current is not None:
            done.append(current)
    return done


def swap_chunks(tiles):
    tiles = list(tiles)
    chunk = lax.broadcasted_iota(jnp.int32, tiles[0].shape, tiles[0].ndim - 1) // 8
    for bit in (1, 2, 4, 8):
        clear = (chunk & bit) == 0
        for i in range(16):
            if i & bit == 0:
                first, second = tiles[i], tiles[i | bit]
                tiles[i] = jnp.where(clear, first, lane_roll(second, 8 * bit))
                tiles[i | bit] = jnp.where(clear, lane_roll(first, -8 * bit), second)
    return tiles


def top_lanes(shape):
    chunk = lax.broadcasted_iota(jnp.int32, shape, len(shape) - 1) // 8
    return (chunk & 4) != 0


def pair_codes(low, high):
    low, high = (jnp.round(v).astype(jnp.int32) for v in (low, high))
    return (high << 16) | (low & 0xFFFF)


def codes_of(word):
    return ((word << 16) >> 16).astype(F32), (word >> 16).astype(F32)


def unit_of(values):
    largest = functools.reduce(jnp.maximum, [jnp.abs(v) for v in values])
    largest = jnp.max(jnp.max(largest, 0, keepdims=True), 1, keepdims=True)
    largest = jnp.maximum(largest, 1e-30)
    return jnp.broadcast_to(largest * (1.0 / LIMIT), (1, LANES)), LIMIT / largest


def kernel(
    n_mem, n_rows,
    x_ref, values_ref, variance_ref, mask_ref, out_ref,
    x_local, values, variance, mask,
    band, band_above, band_below,
    obs, obs_above, obs_below, obs_wide, obs_left, obs_right,
    chunks, regions, unit, units, back_unit, back_units, analysed, edges_up, edges_down, own_part, above_part, below_part,
    token, load_sem, band_send, band_recv, obs_send, obs_recv,
    region_send, region_recv, unit_send, unit_recv, own_send, own_recv, back_send, back_recv, down_send, down_recv, up_send, up_recv,
):
    members = n_mem * 16
    me_mem, me_row = lax.axis_index("mem"), lax.axis_index("rows")
    above, below = lax.rem(me_row + n_rows - 1, n_rows), lax.rem(me_row + 1, n_rows)
    left, right = lax.rem(me_mem + n_mem - 1, n_mem), lax.rem(me_mem + 1, n_mem)

    def at(mem, row):
        return {"mem": mem, "rows": row}

    def remote(src, dst, send, recv, mem, row):
        return pltpu.make_async_remote_copy(
            src_ref=src, dst_ref=dst, send_sem=send, recv_sem=recv,
            device_id=at(mem, row), device_id_type=MESH,
        )

    offsets = sorted(range(1, n_mem), key=lambda d: -min(d, n_mem - d))
    partners = [lax.rem(me_mem + d, n_mem) for d in offsets]

    barrier = pltpu.get_barrier_semaphore()

    def ring(mem, step):
        return lax.rem(mem + step + n_mem, n_mem)

    def greet(semaphore, mem, row):
        pl.semaphore_signal(semaphore, inc=1, device_id=at(mem, row), device_id_type=MESH)

    pair = me_mem + 1 - 2 * lax.rem(me_mem, 2)
    near = [pair] + [ring(mem, step) for mem in (me_mem, pair) for step in (4, -4, 2, -2)]
    for row in (above, below):
        greet(barrier, me_mem, row)
    for mem in near:
        greet(barrier, mem, me_row)

    loads = [
        pltpu.make_async_copy(source, target, load_sem.at[i])
        for i, (source, target) in enumerate(
            [
                (x_ref, x_local),
                (values_ref, values),
                (variance_ref, variance),
                (mask_ref, mask),
            ]
        )
    ]
    for load in loads:
        load.start()
    loads[0].wait()

    def rows_of(ref, r, f):
        return ref.at[pl.ds(f * PATCH + r, 16, stride=2 * PATCH), :]

    own_rows = []
    for r in range(PATCH):
        row = tuple(lane_roll(rows_of(x_local, r, f)[...], RADIUS) for f in range(2))
        own_rows.append(row)
        word = pair_codes(*(value * (LIMIT / BOUND) for value in row))
        for half in range(2):
            band[half, r] = word[8 * half : 8 * half + 8]

    pl.semaphore_wait(barrier, 2 + len(near))

    band_copies = [
        [
            remote(
                band.at[half], part.at[half],
                band_send.at[half, i], band_recv.at[half, i], me_mem, row,
            )
            for i, (part, row) in enumerate([(band_above, below), (band_below, above)])
        ]
        for half in range(2)
    ]
    for copies in band_copies:
        for copy in copies:
            copy.start()
    for step in (4, -4):
        greet(token, ring(me_mem, step), me_row)

    for load in loads[1:]:
        load.wait()
    weight = (mask[...].astype(F32) * variance[...]).astype(BF16).astype(F32)
    planes = jnp.concatenate(
        [weight.reshape(2 * PATCH, PATCH), values[...].reshape(2 * PATCH, PATCH)], 0
    )
    spread = (
        lax.broadcasted_iota(jnp.int32, (PATCH, LANES), 1) % 8
        == lax.broadcasted_iota(jnp.int32, (PATCH, LANES), 0)
    ).astype(F32)
    wide = jnp.dot(planes, spread, precision=HIGHEST, preferred_element_type=F32)
    wide = wide.reshape(4, PATCH, LANES)
    keep = (
        lax.broadcasted_iota(jnp.int32, wide.shape, 2) // 8
        == lax.broadcasted_iota(jnp.int32, wide.shape, 1) + RADIUS
    )
    wide = jnp.sum(jnp.where(keep, wide, 0.0), 1)
    obs[...] = jnp.concatenate([wide, jnp.zeros((4, LANES), F32)], 0)

    obs_copies = [
        remote(obs, obs_above, obs_send.at[0], obs_recv.at[0], me_mem, below),
        remote(obs, obs_below, obs_send.at[1], obs_recv.at[1], me_mem, above),
        remote(obs_wide, obs_left, obs_send.at[2], obs_recv.at[2], right, me_row),
        remote(obs_wide, obs_right, obs_send.at[3], obs_recv.at[3], left, me_row),
    ]
    obs_copies[0].start()
    obs_copies[1].start()


    def rows_in(part, half):
        words = [part[half, r] for r in range(PATCH)]
        return [tuple(v * (BOUND / LIMIT) for v in codes_of(word)) for word in words]

    for half in range(2):
        for copy in band_copies[half]:
            copy.wait_recv()
        rows = rows_in(band_above, half)
        rows += [tuple(v[8 * half : 8 * half + 8] for v in row) for row in own_rows]
        rows += rows_in(band_below, half)
        ready = forecast_rows(rows)
        unit[half], grain = unit_of([v for row in ready for v in row])
        grain = jnp.broadcast_to(grain, (8, LANES))
        tiles = swap_chunks([pair_codes(*(v * grain for v in row)) for row in ready])
        for j in range(n_mem):
            chunks[half, j] = tiles[j]
        chunks[half, n_mem] = tiles[0]

        if half == 0:
            pl.semaphore_wait(token, 2)

        for partner in partners:
            remote(
                chunks.at[half, pl.ds(partner, 2)], regions.at[me_mem, half],
                region_send, region_recv, partner, me_row,
            ).start()
    for partner in partners:
        remote(unit, units.at[me_mem], unit_send, unit_recv, partner, me_row).start()
    for half in range(2):
        regions[me_mem, half] = chunks[half, pl.ds(me_mem, 2)]
    units[me_mem] = unit[...]

    lane = lax.broadcasted_iota(jnp.int32, (8, LANES), 1)
    obs_copies[0].wait_recv()
    obs_copies[1].wait_recv()
    turned = lane_roll(jnp.where(lane >= 64, obs_above[...], obs_below[...]), 64)
    extended = jnp.where((lane >= 32) & (lane < 96), obs[...], turned)
    obs_wide[...] = extended
    obs_copies[2].start()
    obs_copies[3].start()
    obs_copies[2].wait_recv()
    obs_copies[3].wait_recv()
    lower = lane % 8 < 4
    halves = (
        jnp.where(lower, lane_roll(obs_left[...], -4), lane_roll(extended, 4)),
        jnp.where(lower, lane_roll(extended, -4), lane_roll(obs_right[...], 4)),
    )
    order = [(h, f) for h in range(2) for f in range(2)]
    weight_row = jnp.concatenate([halves[h][f : f + 1] for h, f in order], 1)
    value_row = jnp.concatenate([halves[h][2 + f : 3 + f] for h, f in order], 1)
    point = lax.broadcasted_iota(jnp.int32, (1, 4 * LANES), 1)
    region_row = point % LANES // 8
    region_col = point // (2 * LANES) * 8 + point % 8

    def distance(index):
        return jnp.maximum(jnp.maximum(RADIUS - index, index - (RADIUS + PATCH - 1)), 0)

    far = jnp.maximum(distance(region_row), distance(region_col)).astype(F32)
    factor = weight_row * (1.0 - far / (RADIUS + 1.0))

    column = lax.broadcasted_iota(jnp.int32, (4 * LANES, 2 * LANES), 1)
    lane = column % LANES
    turn = jnp.where((lane & 32) != 0, 32, LANES - 32)
    lane = jnp.where(column < LANES, lane, (lane + turn) % LANES)
    field = 1 - ((lane >= 32) & (lane < 96)).astype(jnp.int32)
    grid_row = (lane // 8 + 8 * field) % 16
    grid_col = lane % 8 + RADIUS
    source = (grid_col // 8 * 2 + field) * LANES + grid_row * 8 + grid_col % 8
    select = (lax.broadcasted_iota(jnp.int32, lane.shape, 0) == source).astype(BF16)

    others = n_mem - 1

    def whole(buffer, count, send, recv):
        part = buffer.at[pl.ds(0, count)]
        return remote(part, part, send, recv, right, me_row)

    region_all = whole(regions, others, region_send, region_recv)
    unit_all = whole(units, others, unit_send, unit_recv)
    region_all.wait_recv()
    unit_all.wait_recv()

    every_unit = units[...]
    fields = []
    for h in range(2):
        for code in codes_of(regions[:, :, h]):
            fields.append((code * every_unit).reshape(members, LANES))
    sample = jnp.concatenate(fields, 1)
    mean = jnp.sum(sample, 0, keepdims=True) / members
    deviation = (sample - mean).astype(BF16)
    innovation = (value_row - mean).astype(BF16)
    weighted = (deviation.astype(F32) * factor).astype(BF16)
    inner = jnp.dot(deviation, select, preferred_element_type=F32).astype(BF16)
    stacked = jnp.concatenate(
        [deviation, jnp.broadcast_to(innovation, (16, 4 * LANES))], 0
    )
    product = lax.dot_general(
        stacked, weighted, (((1,), (1,)), ((), ())), preferred_element_type=F32
    )
    gram, projected = product[:members], product[members : members + 8]
    eye = (
        lax.broadcasted_iota(jnp.int32, (members, members), 0)
        == lax.broadcasted_iota(jnp.int32, (members, members), 1)
    ).astype(F32)
    system = (members - 1.0) * eye + gram
    square = jnp.sum(jnp.sum(system * system, 1, keepdims=True), 0, keepdims=True)
    scale = jnp.sqrt(square)

    def mul(a, b):
        return jnp.dot(a.astype(BF16), b.astype(BF16), preferred_element_type=F32)

    y = system * (1.0 / scale)
    y2 = mul(y, y)
    y3 = mul(y, y2)
    y4 = mul(y2, y2)
    y5 = mul(y2, y3)
    zy1 = 2.25 * y - 1.5 * y2 + 0.25 * y3
    zyy1 = 2.25 * y2 - 1.5 * y3 + 0.25 * y4
    zyyy1 = 2.25 * y3 - 1.5 * y4 + 0.25 * y5
    e2 = 0.25 * zyy1 - 0.75 * (y + zy1)
    iter_y = 2.25 * y - 0.75 * (y2 + zyy1) + 0.25 * zyyy1
    zy2 = 2.25 * iter_y + mul(e2, iter_y)
    e3 = 1.5 * e2 - 1.125 * zy2 - 0.5 * mul(zy2, e2)
    lead = (1.5**SCHULZ_STEPS) * eye
    shrink = lax.rsqrt(scale)
    root = (lead + e3) * shrink
    half_way = (1.5**SCHULZ_STEPS) * projected + mul(projected, e3)
    shift = ((1.5**SCHULZ_STEPS) * half_way + mul(half_way, e3)) / scale
    shift = shift[0:1]
    transform = ((members - 1.0) ** 0.5 * root + shift).astype(BF16)

    inner_lane = lax.broadcasted_iota(jnp.int32, (1, LANES), 1)

    def interior(wide_value):
        fields = []
        for f in range(2):
            low = wide_value[:, f * LANES : (f + 1) * LANES]
            high = wide_value[:, (2 + f) * LANES : (3 + f) * LANES]
            fields.append(
                jnp.where(inner_lane % 8 < 4, lane_roll(low, -4), lane_roll(high, 4))
            )
        centre = (inner_lane >= 32) & (inner_lane < 96)
        return jnp.where(centre, fields[0], lane_roll(fields[1], 64))

    increment = jnp.dot(transform, inner, preferred_element_type=F32)
    inner_mean = interior(jnp.broadcast_to(mean, (8, 4 * LANES)))[0:1]
    top = top_lanes((8, LANES))
    mean_rows = jnp.broadcast_to(inner_mean, (8, LANES))
    turned_mean = jnp.where(top, lane_roll(mean_rows, -32), lane_roll(mean_rows, 32))[0:1]
    analysis = inner_mean + increment[:, :LANES]
    turned = turned_mean + increment[:, LANES:]
    parts = (n_mem, 2, 8, LANES)
    first, second = analysis.reshape(parts)[:, 0], turned.reshape(parts)[:, 1]
    top = top_lanes(first.shape)
    edges_up[...] = jnp.where(top, first, second).astype(BF16)
    edges_down[...] = jnp.where(top, second, first).astype(BF16)

    for partner in partners + [me_mem]:
        remote(
            edges_down.at[partner], above_part.at[me_mem], down_send, down_recv, partner, below
        ).start()
        remote(
            edges_up.at[partner], below_part.at[me_mem], up_send, up_recv, partner, above
        ).start()
    back_unit[...], grain = unit_of([analysis])
    scaled = (analysis * grain).reshape(parts)
    analysed[...] = pair_codes(scaled[:, 0], scaled[:, 1])
    for partner in partners:
        remote(
            analysed.at[partner], own_part.at[me_mem], own_send, own_recv, partner, me_row
        ).start()
    for partner in partners:
        remote(
            back_unit, back_units.at[me_mem], back_send, back_recv, partner, me_row
        ).start()
    own_part[me_mem] = analysed[me_mem]
    back_units[me_mem] = back_unit[...]
    for copy in band_copies[0] + band_copies[1] + obs_copies:
        copy.wait_send()
    region_all.wait_send()
    unit_all.wait_send()
    down_all = whole(above_part, n_mem, down_send, down_recv)
    up_all = whole(below_part, n_mem, up_send, up_recv)
    own_all = whole(own_part, others, own_send, own_recv)
    back_all = whole(back_units, others, back_send, back_recv)
    own_all.wait_recv()
    back_all.wait_recv()
    source = lax.broadcasted_iota(jnp.int32, (n_mem, LANES), 0)
    lane = lax.broadcasted_iota(jnp.int32, (n_mem, LANES), 1)
    unit_row = jnp.sum(
        jnp.where(lane // 8 == source, back_units[...].reshape(n_mem, LANES), 0.0),
        0,
        keepdims=True,
    )
    own_tiles = [
        jnp.concatenate([v * unit_row for v in codes_of(tile)], 0)
        for tile in swap_chunks([own_part[j] for j in range(n_mem)])
    ]
    state = [{} for _ in range(FSTEPS + 1)]
    state[0] = {i: (own_tiles[4 + i], own_tiles[(12 + i) % 16]) for i in range(PATCH)}

    def fill(first, last):
        for step in range(1, FSTEPS + 1):
            before, after = state[step - 1], state[step]
            for r in range(first + step, last - step):
                if r not in after:
                    after[r] = advance(before[r - 1], before[r], before[r + 1])

    fill(0, PATCH)
    down_all.wait_recv()
    up_all.wait_recv()
    edge_tiles = swap_chunks(
        [
            jnp.concatenate([below_part[j].astype(F32), above_part[j].astype(F32)], 0)
            for j in range(n_mem)
        ]
    )

    def edge_row(part, first, second):
        pick = slice(8 * part, 8 * part + 8)
        return jnp.concatenate([edge_tiles[first][pick], edge_tiles[second][pick]], 0)

    for i in range(RADIUS):
        state[0][i - RADIUS] = (edge_row(1, 8 + i, 4 + i), edge_row(1, i, 12 + i))
        state[0][i + PATCH] = (edge_row(0, 4 + i, 8 + i), edge_row(0, 12 + i, i))
    fill(-RADIUS, PATCH + RADIUS)
    for r in range(PATCH):
        for f in range(2):
            rows_of(out_ref, r, f)[...] = state[FSTEPS][r][f]

    for copies in (own_all, back_all, down_all, up_all):
        copies.wait_send()


def local(sample_collection, obs_values, obs_inverse_variance, obs_mask):
    n_mem, n_rows = lax.axis_size("mem"), lax.axis_size("rows")
    local_members = sample_collection.shape[0]
    dma = pltpu.SemaphoreType.DMA
    band = (2, PATCH, local_members // 2, LANES)
    flat = (local_members * 2 * PATCH, LANES)
    part = (n_mem, local_members // 2, LANES)
    result = pl.pallas_call(
        functools.partial(kernel, n_mem, n_rows),
        out_shape=pltpu.VMEM(flat, F32),
        in_specs=[pl.BlockSpec(memory_space=pl.ANY)] * 4,
        out_specs=pl.BlockSpec(memory_space=pltpu.VMEM),
        scratch_shapes=[
            pltpu.VMEM(flat, F32),
            pltpu.VMEM(obs_values.shape, F32),
            pltpu.VMEM(obs_values.shape, F32),
            pltpu.VMEM(obs_values.shape, jnp.int32),
        ]
        + [pltpu.VMEM(band, jnp.int32)] * 3
        + [pltpu.VMEM((8, LANES), F32)] * 6
        + [
            pltpu.VMEM((2, n_mem + 1, 8, LANES), jnp.int32),
            pltpu.VMEM((n_mem, 2, 2, 8, LANES), jnp.int32),
            pltpu.VMEM((2, 1, LANES), F32),
            pltpu.VMEM((n_mem, 2, 1, LANES), F32),
            pltpu.VMEM((1, LANES), F32),
            pltpu.VMEM((n_mem, 1, LANES), F32),
            pltpu.VMEM(part, jnp.int32),
            pltpu.VMEM(part, BF16),
            pltpu.VMEM(part, BF16),
            pltpu.VMEM(part, jnp.int32),
            pltpu.VMEM(part, BF16),
            pltpu.VMEM(part, BF16),
        ]
        + [pltpu.SemaphoreType.REGULAR]
        + [dma((4,)), dma((2, 2)), dma((2, 2)), dma((4,)), dma((4,))]
        + [dma(())] * 12,
        compiler_params=pltpu.CompilerParams(collective_id=0, has_side_effects=True),
    )(
        sample_collection.reshape(flat),
        obs_values,
        obs_inverse_variance,
        obs_mask,
    )
    return result.reshape(sample_collection.shape)


def solution(mesh):
    return jax.shard_map(
        local,
        mesh=mesh,
        in_specs=(
            P("mem", None, "rows", None),
            P(None, "rows", "mem"),
            P(None, "rows", "mem"),
            P(None, "rows", "mem"),
        ),
        out_specs=P("mem", None, "rows", None),
        check_vma=False,
    )
```

```python
import functools

import jax
import jax.numpy as jnp
from jax import lax
from jax.experimental import pallas as pl
from jax.experimental.pallas import tpu as pltpu
from jax.sharding import PartitionSpec as P

PATCH = 8
RADIUS = 4
FSTEPS = 4
SCHULZ_STEPS = 3
CADV = 0.05
LANES = 128
MESH = pl.DeviceIdType.MESH
HIGHEST = lax.Precision.HIGHEST
BF16 = jnp.bfloat16
F32 = jnp.float32
LIMIT = 32766.0
BOUND = 6.0


def lane_roll(value, shift):
    return pltpu.roll(value, shift % LANES, value.ndim - 1)


def advance(above, here, below):
    u_field, v_field = here

    def tendency(f):
        along_x = lane_roll(here[f], -1) - lane_roll(here[f], 1)
        along_y = below[f] - above[f]
        return here[f] - CADV * (u_field * along_x + v_field * along_y)

    return tendency(0), tendency(1)


def forecast_rows(rows):
    history = [[] for _ in range(FSTEPS)]
    done = []
    for row in rows:
        current = row
        for level in history:
            level.append(current)
            if len(level) < 3:
                current = None
                break
            current = advance(*level[-3:])
        if current is not None:
            done.append(current)
    return done


def swap_chunks(tiles):
    tiles = list(tiles)
    chunk = lax.broadcasted_iota(jnp.int32, tiles[0].shape, tiles[0].ndim - 1) // 8
    for bit in (1, 2, 4, 8):
        clear = (chunk & bit) == 0
        for i in range(16):
            if i & bit == 0:
                first, second = tiles[i], tiles[i | bit]
                tiles[i] = jnp.where(clear, first, lane_roll(second, 8 * bit))
                tiles[i | bit] = jnp.where(clear, lane_roll(first, -8 * bit), second)
    return tiles


def top_lanes(shape):
    chunk = lax.broadcasted_iota(jnp.int32, shape, len(shape) - 1) // 8
    return (chunk & 4) != 0


def pair_codes(low, high):
    low, high = (jnp.round(v).astype(jnp.int32) for v in (low, high))
    return (high << 16) | (low & 0xFFFF)


def codes_of(word):
    return ((word << 16) >> 16).astype(F32), (word >> 16).astype(F32)


def unit_of(values):
    largest = functools.reduce(jnp.maximum, [jnp.abs(v) for v in values])
    largest = jnp.max(jnp.max(largest, 0, keepdims=True), 1, keepdims=True)
    largest = jnp.maximum(largest, 1e-30)
    return jnp.broadcast_to(largest * (1.0 / LIMIT), (1, LANES)), LIMIT / largest


def kernel(
    n_mem, n_rows,
    x_ref, values_ref, variance_ref, mask_ref, out_ref,
    x_local, values, variance, mask,
    band, band_above, band_below,
    obs, obs_above, obs_below, obs_wide, obs_left, obs_right,
    chunks, regions, unit, units, back_unit, back_units, analysed, edges_up, edges_down, own_part, above_part, below_part,
    token, load_sem, band_send, band_recv, obs_send, obs_recv,
    region_send, region_recv, unit_send, unit_recv, own_send, own_recv, back_send, back_recv, down_send, down_recv, up_send, up_recv,
):
    members = n_mem * 16
    me_mem, me_row = lax.axis_index("mem"), lax.axis_index("rows")
    above, below = lax.rem(me_row + n_rows - 1, n_rows), lax.rem(me_row + 1, n_rows)
    left, right = lax.rem(me_mem + n_mem - 1, n_mem), lax.rem(me_mem + 1, n_mem)

    def at(mem, row):
        return {"mem": mem, "rows": row}

    def remote(src, dst, send, recv, mem, row):
        return pltpu.make_async_remote_copy(
            src_ref=src, dst_ref=dst, send_sem=send, recv_sem=recv,
            device_id=at(mem, row), device_id_type=MESH,
        )

    offsets = sorted(range(1, n_mem), key=lambda d: -min(d, n_mem - d))
    partners = [lax.rem(me_mem + d, n_mem) for d in offsets]

    loads = [
        pltpu.make_async_copy(source, target, load_sem.at[i])
        for i, (source, target) in enumerate(
            [
                (x_ref, x_local),
                (values_ref, values),
                (variance_ref, variance),
                (mask_ref, mask),
            ]
        )
    ]
    loads[0].start()

    barrier = pltpu.get_barrier_semaphore()

    def ring(mem, step):
        return lax.rem(mem + step + n_mem, n_mem)

    def greet(semaphore, mem, row):
        pl.semaphore_signal(semaphore, inc=1, device_id=at(mem, row), device_id_type=MESH)

    pair = me_mem + 1 - 2 * lax.rem(me_mem, 2)
    near = [pair] + [ring(mem, step) for mem in (me_mem, pair) for step in (4, -4, 2, -2)]
    distant = [ring(mem, step) for step in (8, 6, -6) for mem in (me_mem, pair)]
    for row in (above, below):
        greet(barrier, me_mem, row)
    for mem in near:
        greet(barrier, mem, me_row)

    for load in loads[1:]:
        load.start()
    loads[0].wait()

    def rows_of(ref, r, f):
        return ref.at[pl.ds(f * PATCH + r, 16, stride=2 * PATCH), :]

    own_rows = []
    for r in range(PATCH):
        row = tuple(lane_roll(rows_of(x_local, r, f)[...], RADIUS) for f in range(2))
        own_rows.append(row)
        word = pair_codes(*(value * (LIMIT / BOUND) for value in row))
        for half in range(2):
            band[half, r] = word[8 * half : 8 * half + 8]

    pl.semaphore_wait(barrier, 2 + len(near))

    band_copies = [
        [
            remote(
                band.at[half], part.at[half],
                band_send.at[half, i], band_recv.at[half, i], me_mem, row,
            )
            for i, (part, row) in enumerate([(band_above, below), (band_below, above)])
        ]
        for half in range(2)
    ]
    for copies in band_copies:
        for copy in copies:
            copy.start()
    for step in (4, -4):
        greet(token, ring(me_mem, step), me_row)

    for load in loads[1:]:
        load.wait()
    weight = (mask[...].astype(F32) * variance[...]).astype(BF16).astype(F32)
    planes = jnp.concatenate(
        [weight.reshape(2 * PATCH, PATCH), values[...].reshape(2 * PATCH, PATCH)], 0
    )
    spread = (
        lax.broadcasted_iota(jnp.int32, (PATCH, LANES), 1) % 8
        == lax.broadcasted_iota(jnp.int32, (PATCH, LANES), 0)
    ).astype(F32)
    wide = jnp.dot(planes, spread, precision=HIGHEST, preferred_element_type=F32)
    wide = wide.reshape(4, PATCH, LANES)
    keep = (
        lax.broadcasted_iota(jnp.int32, wide.shape, 2) // 8
        == lax.broadcasted_iota(jnp.int32, wide.shape, 1) + RADIUS
    )
    wide = jnp.sum(jnp.where(keep, wide, 0.0), 1)
    obs[...] = jnp.concatenate([wide, jnp.zeros((4, LANES), F32)], 0)

    obs_copies = [
        remote(obs, obs_above, obs_send.at[0], obs_recv.at[0], me_mem, below),
        remote(obs, obs_below, obs_send.at[1], obs_recv.at[1], me_mem, above),
        remote(obs_wide, obs_left, obs_send.at[2], obs_recv.at[2], right, me_row),
        remote(obs_wide, obs_right, obs_send.at[3], obs_recv.at[3], left, me_row),
    ]
    obs_copies[0].start()
    obs_copies[1].start()


    def rows_in(part, half):
        words = [part[half, r] for r in range(PATCH)]
        return [tuple(v * (BOUND / LIMIT) for v in codes_of(word)) for word in words]

    for half in range(2):
        for copy in band_copies[half]:
            copy.wait_recv()
        rows = rows_in(band_above, half)
        rows += [tuple(v[8 * half : 8 * half + 8] for v in row) for row in own_rows]
        rows += rows_in(band_below, half)
        ready = forecast_rows(rows)
        unit[half], grain = unit_of([v for row in ready for v in row])
        grain = jnp.broadcast_to(grain, (8, LANES))
        tiles = swap_chunks([pair_codes(*(v * grain for v in row)) for row in ready])
        for j in range(n_mem):
            chunks[half, j] = tiles[j]
        chunks[half, n_mem] = tiles[0]

        def send(partner):
            remote(
                chunks.at[half, pl.ds(partner, 2)], regions.at[me_mem, half],
                region_send, region_recv, partner, me_row,
            ).start()

        if half == 0:
            for partner in near:
                send(partner)
            pl.semaphore_wait(token, 2)
            for partner in distant:
                send(partner)
        else:
            for partner in partners:
                send(partner)
    for partner in partners:
        remote(unit, units.at[me_mem], unit_send, unit_recv, partner, me_row).start()
    for half in range(2):
        regions[me_mem, half] = chunks[half, pl.ds(me_mem, 2)]
    units[me_mem] = unit[...]

    lane = lax.broadcasted_iota(jnp.int32, (8, LANES), 1)
    obs_copies[0].wait_recv()
    obs_copies[1].wait_recv()
    turned = lane_roll(jnp.where(lane >= 64, obs_above[...], obs_below[...]), 64)
    extended = jnp.where((lane >= 32) & (lane < 96), obs[...], turned)
    obs_wide[...] = extended
    obs_copies[2].start()
    obs_copies[3].start()
    obs_copies[2].wait_recv()
    obs_copies[3].wait_recv()
    lower = lane % 8 < 4
    halves = (
        jnp.where(lower, lane_roll(obs_left[...], -4), lane_roll(extended, 4)),
        jnp.where(lower, lane_roll(extended, -4), lane_roll(obs_right[...], 4)),
    )
    order = [(h, f) for h in range(2) for f in range(2)]
    weight_row = jnp.concatenate([halves[h][f : f + 1] for h, f in order], 1)
    value_row = jnp.concatenate([halves[h][2 + f : 3 + f] for h, f in order], 1)
    point = lax.broadcasted_iota(jnp.int32, (1, 4 * LANES), 1)
    region_row = point % LANES // 8
    region_col = point // (2 * LANES) * 8 + point % 8

    def distance(index):
        return jnp.maximum(jnp.maximum(RADIUS - index, index - (RADIUS + PATCH - 1)), 0)

    far = jnp.maximum(distance(region_row), distance(region_col)).astype(F32)
    factor = weight_row * (1.0 - far / (RADIUS + 1.0))

    column = lax.broadcasted_iota(jnp.int32, (4 * LANES, 2 * LANES), 1)
    lane = column % LANES
    turn = jnp.where((lane & 32) != 0, 32, LANES - 32)
    lane = jnp.where(column < LANES, lane, (lane + turn) % LANES)
    field = 1 - ((lane >= 32) & (lane < 96)).astype(jnp.int32)
    grid_row = (lane // 8 + 8 * field) % 16
    grid_col = lane % 8 + RADIUS
    source = (grid_col // 8 * 2 + field) * LANES + grid_row * 8 + grid_col % 8
    select = (lax.broadcasted_iota(jnp.int32, lane.shape, 0) == source).astype(BF16)

    others = n_mem - 1

    def whole(buffer, count, send, recv):
        part = buffer.at[pl.ds(0, count)]
        return remote(part, part, send, recv, right, me_row)

    region_all = whole(regions, others, region_send, region_recv)
    unit_all = whole(units, others, unit_send, unit_recv)
    region_all.wait_recv()
    unit_all.wait_recv()

    every_unit = units[...]
    fields = []
    for h in range(2):
        for code in codes_of(regions[:, :, h]):
            fields.append((code * every_unit).reshape(members, LANES))
    sample = jnp.concatenate(fields, 1)
    mean = jnp.sum(sample, 0, keepdims=True) / members
    deviation = (sample - mean).astype(BF16)
    innovation = (value_row - mean).astype(BF16)
    weighted = (deviation.astype(F32) * factor).astype(BF16)
    inner = jnp.dot(deviation, select, preferred_element_type=F32).astype(BF16)
    stacked = jnp.concatenate(
        [deviation, jnp.broadcast_to(innovation, (16, 4 * LANES))], 0
    )
    product = lax.dot_general(
        stacked, weighted, (((1,), (1,)), ((), ())), preferred_element_type=F32
    )
    gram, projected = product[:members], product[members : members + 8]
    eye = (
        lax.broadcasted_iota(jnp.int32, (members, members), 0)
        == lax.broadcasted_iota(jnp.int32, (members, members), 1)
    ).astype(F32)
    system = (members - 1.0) * eye + gram
    square = jnp.sum(jnp.sum(system * system, 1, keepdims=True), 0, keepdims=True)
    scale = jnp.sqrt(square)

    def mul(a, b):
        return jnp.dot(a.astype(BF16), b.astype(BF16), preferred_element_type=F32)

    y = system * (1.0 / scale)
    y2 = mul(y, y)
    y3 = mul(y, y2)
    y4 = mul(y2, y2)
    y5 = mul(y2, y3)
    zy1 = 2.25 * y - 1.5 * y2 + 0.25 * y3
    zyy1 = 2.25 * y2 - 1.5 * y3 + 0.25 * y4
    zyyy1 = 2.25 * y3 - 1.5 * y4 + 0.25 * y5
    e2 = 0.25 * zyy1 - 0.75 * (y + zy1)
    iter_y = 2.25 * y - 0.75 * (y2 + zyy1) + 0.25 * zyyy1
    zy2 = 2.25 * iter_y + mul(e2, iter_y)
    e3 = 1.5 * e2 - 1.125 * zy2 - 0.5 * mul(zy2, e2)
    lead = (1.5**SCHULZ_STEPS) * eye
    shrink = lax.rsqrt(scale)
    root = (lead + e3) * shrink
    half_way = (1.5**SCHULZ_STEPS) * projected + mul(projected, e3)
    shift = ((1.5**SCHULZ_STEPS) * half_way + mul(half_way, e3)) / scale
    shift = shift[0:1]
    transform = ((members - 1.0) ** 0.5 * root + shift).astype(BF16)

    inner_lane = lax.broadcasted_iota(jnp.int32, (1, LANES), 1)

    def interior(wide_value):
        fields = []
        for f in range(2):
            low = wide_value[:, f * LANES : (f + 1) * LANES]
            high = wide_value[:, (2 + f) * LANES : (3 + f) * LANES]
            fields.append(
                jnp.where(inner_lane % 8 < 4, lane_roll(low, -4), lane_roll(high, 4))
            )
        centre = (inner_lane >= 32) & (inner_lane < 96)
        return jnp.where(centre, fields[0], lane_roll(fields[1], 64))

    increment = jnp.dot(transform, inner, preferred_element_type=F32)
    inner_mean = interior(jnp.broadcast_to(mean, (8, 4 * LANES)))[0:1]
    top = top_lanes((8, LANES))
    mean_rows = jnp.broadcast_to(inner_mean, (8, LANES))
    turned_mean = jnp.where(top, lane_roll(mean_rows, -32), lane_roll(mean_rows, 32))[0:1]
    analysis = inner_mean + increment[:, :LANES]
    turned = turned_mean + increment[:, LANES:]
    parts = (n_mem, 2, 8, LANES)
    first, second = analysis.reshape(parts)[:, 0], turned.reshape(parts)[:, 1]
    top = top_lanes(first.shape)
    edges_up[...] = jnp.where(top, first, second).astype(BF16)
    edges_down[...] = jnp.where(top, second, first).astype(BF16)

    for partner in partners + [me_mem]:
        remote(
            edges_down.at[partner], above_part.at[me_mem], down_send, down_recv, partner, below
        ).start()
        remote(
            edges_up.at[partner], below_part.at[me_mem], up_send, up_recv, partner, above
        ).start()
    back_unit[...], grain = unit_of([analysis])
    scaled = (analysis * grain).reshape(parts)
    analysed[...] = pair_codes(scaled[:, 0], scaled[:, 1])
    for partner in partners:
        remote(
            analysed.at[partner], own_part.at[me_mem], own_send, own_recv, partner, me_row
        ).start()
    for partner in partners:
        remote(
            back_unit, back_units.at[me_mem], back_send, back_recv, partner, me_row
        ).start()
    own_part[me_mem] = analysed[me_mem]
    back_units[me_mem] = back_unit[...]
    for copy in band_copies[0] + band_copies[1] + obs_copies:
        copy.wait_send()
    region_all.wait_send()
    unit_all.wait_send()
    down_all = whole(above_part, n_mem, down_send, down_recv)
    up_all = whole(below_part, n_mem, up_send, up_recv)
    own_all = whole(own_part, others, own_send, own_recv)
    back_all = whole(back_units, others, back_send, back_recv)
    own_all.wait_recv()
    back_all.wait_recv()
    source = lax.broadcasted_iota(jnp.int32, (n_mem, LANES), 0)
    lane = lax.broadcasted_iota(jnp.int32, (n_mem, LANES), 1)
    unit_row = jnp.sum(
        jnp.where(lane // 8 == source, back_units[...].reshape(n_mem, LANES), 0.0),
        0,
        keepdims=True,
    )
    own_tiles = [
        jnp.concatenate([v * unit_row for v in codes_of(tile)], 0)
        for tile in swap_chunks([own_part[j] for j in range(n_mem)])
    ]
    state = [{} for _ in range(FSTEPS + 1)]
    state[0] = {i: (own_tiles[4 + i], own_tiles[(12 + i) % 16]) for i in range(PATCH)}

    def fill(first, last):
        for step in range(1, FSTEPS + 1):
            before, after = state[step - 1], state[step]
            for r in range(first + step, last - step):
                if r not in after:
                    after[r] = advance(before[r - 1], before[r], before[r + 1])

    fill(0, PATCH)
    down_all.wait_recv()
    up_all.wait_recv()
    edge_tiles = swap_chunks(
        [
            jnp.concatenate([below_part[j].astype(F32), above_part[j].astype(F32)], 0)
            for j in range(n_mem)
        ]
    )

    def edge_row(part, first, second):
        pick = slice(8 * part, 8 * part + 8)
        return jnp.concatenate([edge_tiles[first][pick], edge_tiles[second][pick]], 0)

    for i in range(RADIUS):
        state[0][i - RADIUS] = (edge_row(1, 8 + i, 4 + i), edge_row(1, i, 12 + i))
        state[0][i + PATCH] = (edge_row(0, 4 + i, 8 + i), edge_row(0, 12 + i, i))
    fill(-RADIUS, PATCH + RADIUS)
    for r in range(PATCH):
        for f in range(2):
            rows_of(out_ref, r, f)[...] = state[FSTEPS][r][f]

    for copies in (own_all, back_all, down_all, up_all):
        copies.wait_send()


def local(sample_collection, obs_values, obs_inverse_variance, obs_mask):
    n_mem, n_rows = lax.axis_size("mem"), lax.axis_size("rows")
    local_members = sample_collection.shape[0]
    dma = pltpu.SemaphoreType.DMA
    band = (2, PATCH, local_members // 2, LANES)
    flat = (local_members * 2 * PATCH, LANES)
    part = (n_mem, local_members // 2, LANES)
    result = pl.pallas_call(
        functools.partial(kernel, n_mem, n_rows),
        out_shape=pltpu.VMEM(flat, F32),
        in_specs=[pl.BlockSpec(memory_space=pl.ANY)] * 4,
        out_specs=pl.BlockSpec(memory_space=pltpu.VMEM),
        scratch_shapes=[
            pltpu.VMEM(flat, F32),
            pltpu.VMEM(obs_values.shape, F32),
            pltpu.VMEM(obs_values.shape, F32),
            pltpu.VMEM(obs_values.shape, jnp.int32),
        ]
        + [pltpu.VMEM(band, jnp.int32)] * 3
        + [pltpu.VMEM((8, LANES), F32)] * 6
        + [
            pltpu.VMEM((2, n_mem + 1, 8, LANES), jnp.int32),
            pltpu.VMEM((n_mem, 2, 2, 8, LANES), jnp.int32),
            pltpu.VMEM((2, 1, LANES), F32),
            pltpu.VMEM((n_mem, 2, 1, LANES), F32),
            pltpu.VMEM((1, LANES), F32),
            pltpu.VMEM((n_mem, 1, LANES), F32),
            pltpu.VMEM(part, jnp.int32),
            pltpu.VMEM(part, BF16),
            pltpu.VMEM(part, BF16),
            pltpu.VMEM(part, jnp.int32),
            pltpu.VMEM(part, BF16),
            pltpu.VMEM(part, BF16),
        ]
        + [pltpu.SemaphoreType.REGULAR]
        + [dma((4,)), dma((2, 2)), dma((2, 2)), dma((4,)), dma((4,))]
        + [dma(())] * 12,
        compiler_params=pltpu.CompilerParams(collective_id=0, has_side_effects=True),
    )(
        sample_collection.reshape(flat),
        obs_values,
        obs_inverse_variance,
        obs_mask,
    )
    return result.reshape(sample_collection.shape)


def solution(mesh):
    return jax.shard_map(
        local,
        mesh=mesh,
        in_specs=(
            P("mem", None, "rows", None),
            P(None, "rows", "mem"),
            P(None, "rows", "mem"),
            P(None, "rows", "mem"),
        ),
        out_specs=P("mem", None, "rows", None),
        check_vma=False,
    )
```

```python
import functools

import jax
import jax.numpy as jnp
from jax import lax
from jax.experimental import pallas as pl
from jax.experimental.pallas import tpu as pltpu
from jax.sharding import PartitionSpec as P

PATCH = 8
RADIUS = 4
FSTEPS = 4
SCHULZ_STEPS = 3
CADV = 0.05
LANES = 128
MESH = pl.DeviceIdType.MESH
HIGHEST = lax.Precision.HIGHEST
BF16 = jnp.bfloat16
F32 = jnp.float32
LIMIT = 32766.0
BOUND = 6.0


def lane_roll(value, shift):
    return pltpu.roll(value, shift % LANES, value.ndim - 1)


def advance(above, here, below):
    u_field, v_field = here

    def tendency(f):
        along_x = lane_roll(here[f], -1) - lane_roll(here[f], 1)
        along_y = below[f] - above[f]
        return here[f] - CADV * (u_field * along_x + v_field * along_y)

    return tendency(0), tendency(1)


def forecast_rows(rows):
    history = [[] for _ in range(FSTEPS)]
    done = []
    for row in rows:
        current = row
        for level in history:
            level.append(current)
            if len(level) < 3:
                current = None
                break
            current = advance(*level[-3:])
        if current is not None:
            done.append(current)
    return done


def swap_chunks(tiles):
    tiles = list(tiles)
    chunk = lax.broadcasted_iota(jnp.int32, tiles[0].shape, tiles[0].ndim - 1) // 8
    for bit in (1, 2, 4, 8):
        clear = (chunk & bit) == 0
        for i in range(16):
            if i & bit == 0:
                first, second = tiles[i], tiles[i | bit]
                tiles[i] = jnp.where(clear, first, lane_roll(second, 8 * bit))
                tiles[i | bit] = jnp.where(clear, lane_roll(first, -8 * bit), second)
    return tiles


def top_lanes(shape):
    chunk = lax.broadcasted_iota(jnp.int32, shape, len(shape) - 1) // 8
    return (chunk & 4) != 0


def pair_codes(low, high):
    low, high = (jnp.round(v).astype(jnp.int32) for v in (low, high))
    return (high << 16) | (low & 0xFFFF)


def codes_of(word):
    return ((word << 16) >> 16).astype(F32), (word >> 16).astype(F32)


def unit_of(values):
    largest = functools.reduce(jnp.maximum, [jnp.abs(v) for v in values])
    largest = jnp.max(jnp.max(largest, 0, keepdims=True), 1, keepdims=True)
    largest = jnp.maximum(largest, 1e-30)
    return jnp.broadcast_to(largest * (1.0 / LIMIT), (1, LANES)), LIMIT / largest


def kernel(
    n_mem, n_rows,
    x_ref, values_ref, variance_ref, mask_ref, out_ref,
    x_local, values, variance, mask,
    band, band_above, band_below,
    obs, obs_above, obs_below, obs_wide, obs_left, obs_right,
    chunks, regions, unit, units, back_unit, back_units, analysed, edges_up, edges_down, own_part, above_part, below_part,
    token, load_sem, band_send, band_recv, obs_send, obs_recv,
    region_send, region_recv, unit_send, unit_recv, own_send, own_recv, back_send, back_recv, down_send, down_recv, up_send, up_recv,
):
    members = n_mem * 16
    me_mem, me_row = lax.axis_index("mem"), lax.axis_index("rows")
    above, below = lax.rem(me_row + n_rows - 1, n_rows), lax.rem(me_row + 1, n_rows)
    left, right = lax.rem(me_mem + n_mem - 1, n_mem), lax.rem(me_mem + 1, n_mem)

    def at(mem, row):
        return {"mem": mem, "rows": row}

    def remote(src, dst, send, recv, mem, row):
        return pltpu.make_async_remote_copy(
            src_ref=src, dst_ref=dst, send_sem=send, recv_sem=recv,
            device_id=at(mem, row), device_id_type=MESH,
        )

    offsets = sorted(range(1, n_mem), key=lambda d: -min(d, n_mem - d))
    partners = [lax.rem(me_mem + d, n_mem) for d in offsets]

    loads = [
        pltpu.make_async_copy(source, target, load_sem.at[i])
        for i, (source, target) in enumerate(
            [
                (x_ref, x_local),
                (values_ref, values),
                (variance_ref, variance),
                (mask_ref, mask),
            ]
        )
    ]
    loads[0].start()

    barrier = pltpu.get_barrier_semaphore()

    def ring(mem, step):
        return lax.rem(mem + step + n_mem, n_mem)

    def greet(semaphore, mem, row):
        pl.semaphore_signal(semaphore, inc=1, device_id=at(mem, row), device_id_type=MESH)

    pair = me_mem + 1 - 2 * lax.rem(me_mem, 2)
    near = [pair] + [ring(mem, step) for mem in (me_mem, pair) for step in (4, -4, 2, -2)]
    for row in (above, below):
        greet(barrier, me_mem, row)
    for mem in near:
        greet(barrier, mem, me_row)

    for load in loads[1:]:
        load.start()
    loads[0].wait()

    def rows_of(ref, r, f):
        return ref.at[pl.ds(f * PATCH + r, 16, stride=2 * PATCH), :]

    own_rows = []
    for r in range(PATCH):
        row = tuple(lane_roll(rows_of(x_local, r, f)[...], RADIUS) for f in range(2))
        own_rows.append(row)
        word = pair_codes(*(value * (LIMIT / BOUND) for value in row))
        for half in range(2):
            band[half, r] = word[8 * half : 8 * half + 8]

    pl.semaphore_wait(barrier, 2 + len(near))

    band_copies = [
        [
            remote(
                band.at[half], part.at[half],
                band_send.at[half, i], band_recv.at[half, i], me_mem, row,
            )
            for i, (part, row) in enumerate([(band_above, below), (band_below, above)])
        ]
        for half in range(2)
    ]
    for copies in band_copies:
        for copy in copies:
            copy.start()
    for step in (4, -4):
        greet(token, ring(me_mem, step), me_row)

    for load in loads[1:]:
        load.wait()
    weight = (mask[...].astype(F32) * variance[...]).astype(BF16).astype(F32)
    planes = jnp.concatenate(
        [weight.reshape(2 * PATCH, PATCH), values[...].reshape(2 * PATCH, PATCH)], 0
    )
    spread = (
        lax.broadcasted_iota(jnp.int32, (PATCH, LANES), 1) % 8
        == lax.broadcasted_iota(jnp.int32, (PATCH, LANES), 0)
    ).astype(F32)
    wide = jnp.dot(planes, spread, precision=HIGHEST, preferred_element_type=F32)
    wide = wide.reshape(4, PATCH, LANES)
    keep = (
        lax.broadcasted_iota(jnp.int32, wide.shape, 2) // 8
        == lax.broadcasted_iota(jnp.int32, wide.shape, 1) + RADIUS
    )
    wide = jnp.sum(jnp.where(keep, wide, 0.0), 1)
    obs[...] = jnp.concatenate([wide, jnp.zeros((4, LANES), F32)], 0)

    obs_copies = [
        remote(obs, obs_above, obs_send.at[0], obs_recv.at[0], me_mem, below),
        remote(obs, obs_below, obs_send.at[1], obs_recv.at[1], me_mem, above),
        remote(obs_wide, obs_left, obs_send.at[2], obs_recv.at[2], right, me_row),
        remote(obs_wide, obs_right, obs_send.at[3], obs_recv.at[3], left, me_row),
    ]
    obs_copies[0].start()
    obs_copies[1].start()


    def rows_in(part, half):
        words = [part[half, r] for r in range(PATCH)]
        return [tuple(v * (BOUND / LIMIT) for v in codes_of(word)) for word in words]

    for half in range(2):
        for copy in band_copies[half]:
            copy.wait_recv()
        rows = rows_in(band_above, half)
        rows += [tuple(v[8 * half : 8 * half + 8] for v in row) for row in own_rows]
        rows += rows_in(band_below, half)
        ready = forecast_rows(rows)
        unit[half], grain = unit_of([v for row in ready for v in row])
        grain = jnp.broadcast_to(grain, (8, LANES))
        tiles = swap_chunks([pair_codes(*(v * grain for v in row)) for row in ready])
        for j in range(n_mem):
            chunks[half, j] = tiles[j]
        chunks[half, n_mem] = tiles[0]

        if half == 0:
            pl.semaphore_wait(token, 2)

        for partner in partners:
            remote(
                chunks.at[half, pl.ds(partner, 2)], regions.at[me_mem, half],
                region_send, region_recv, partner, me_row,
            ).start()
    for partner in partners:
        remote(unit, units.at[me_mem], unit_send, unit_recv, partner, me_row).start()
    for half in range(2):
        regions[me_mem, half] = chunks[half, pl.ds(me_mem, 2)]
    units[me_mem] = unit[...]

    lane = lax.broadcasted_iota(jnp.int32, (8, LANES), 1)
    obs_copies[0].wait_recv()
    obs_copies[1].wait_recv()
    turned = lane_roll(jnp.where(lane >= 64, obs_above[...], obs_below[...]), 64)
    extended = jnp.where((lane >= 32) & (lane < 96), obs[...], turned)
    obs_wide[...] = extended
    obs_copies[2].start()
    obs_copies[3].start()
    obs_copies[2].wait_recv()
    obs_copies[3].wait_recv()
    lower = lane % 8 < 4
    halves = (
        jnp.where(lower, lane_roll(obs_left[...], -4), lane_roll(extended, 4)),
        jnp.where(lower, lane_roll(extended, -4), lane_roll(obs_right[...], 4)),
    )
    order = [(h, f) for h in range(2) for f in range(2)]
    weight_row = jnp.concatenate([halves[h][f : f + 1] for h, f in order], 1)
    value_row = jnp.concatenate([halves[h][2 + f : 3 + f] for h, f in order], 1)
    point = lax.broadcasted_iota(jnp.int32, (1, 4 * LANES), 1)
    region_row = point % LANES // 8
    region_col = point // (2 * LANES) * 8 + point % 8

    def distance(index):
        return jnp.maximum(jnp.maximum(RADIUS - index, index - (RADIUS + PATCH - 1)), 0)

    far = jnp.maximum(distance(region_row), distance(region_col)).astype(F32)
    factor = weight_row * (1.0 - far / (RADIUS + 1.0))

    column = lax.broadcasted_iota(jnp.int32, (4 * LANES, 2 * LANES), 1)
    lane = column % LANES
    turn = jnp.where((lane & 32) != 0, 32, LANES - 32)
    lane = jnp.where(column < LANES, lane, (lane + turn) % LANES)
    field = 1 - ((lane >= 32) & (lane < 96)).astype(jnp.int32)
    grid_row = (lane // 8 + 8 * field) % 16
    grid_col = lane % 8 + RADIUS
    source = (grid_col // 8 * 2 + field) * LANES + grid_row * 8 + grid_col % 8
    select = (lax.broadcasted_iota(jnp.int32, lane.shape, 0) == source).astype(BF16)

    others = n_mem - 1

    def whole(buffer, count, send, recv):
        part = buffer.at[pl.ds(0, count)]
        return remote(part, part, send, recv, right, me_row)

    region_all = whole(regions, others, region_send, region_recv)
    unit_all = whole(units, others, unit_send, unit_recv)
    region_all.wait_recv()
    unit_all.wait_recv()

    every_unit = units[...]
    fields = []
    for h in range(2):
        for code in codes_of(regions[:, :, h]):
            fields.append((code * every_unit).reshape(members, LANES))
    sample = jnp.concatenate(fields, 1)
    mean = jnp.sum(sample, 0, keepdims=True) / members
    deviation = (sample - mean).astype(BF16)
    innovation = (value_row - mean).astype(BF16)
    weighted = (deviation.astype(F32) * factor).astype(BF16)
    inner = jnp.dot(deviation, select, preferred_element_type=F32).astype(BF16)
    stacked = jnp.concatenate(
        [deviation, jnp.broadcast_to(innovation, (16, 4 * LANES))], 0
    )
    product = lax.dot_general(
        stacked, weighted, (((1,), (1,)), ((), ())), preferred_element_type=F32
    )
    gram, projected = product[:members], product[members : members + 8]
    eye = (
        lax.broadcasted_iota(jnp.int32, (members, members), 0)
        == lax.broadcasted_iota(jnp.int32, (members, members), 1)
    ).astype(F32)
    system = (members - 1.0) * eye + gram
    square = jnp.sum(jnp.sum(system * system, 1, keepdims=True), 0, keepdims=True)
    scale = jnp.sqrt(square)

    def mul(a, b):
        return jnp.dot(a.astype(BF16), b.astype(BF16), preferred_element_type=F32)

    y = system * (1.0 / scale)
    y2 = mul(y, y)
    y3 = mul(y, y2)
    y4 = mul(y2, y2)
    y5 = mul(y2, y3)
    zy1 = 2.25 * y - 1.5 * y2 + 0.25 * y3
    zyy1 = 2.25 * y2 - 1.5 * y3 + 0.25 * y4
    zyyy1 = 2.25 * y3 - 1.5 * y4 + 0.25 * y5
    e2 = 0.25 * zyy1 - 0.75 * (y + zy1)
    iter_y = 2.25 * y - 0.75 * (y2 + zyy1) + 0.25 * zyyy1
    zy2 = 2.25 * iter_y + mul(e2, iter_y)
    e3 = 1.5 * e2 - 1.125 * zy2 - 0.5 * mul(zy2, e2)
    lead = (1.5**SCHULZ_STEPS) * eye
    shrink = lax.rsqrt(scale)
    root = (lead + e3) * shrink
    half_way = (1.5**SCHULZ_STEPS) * projected + mul(projected, e3)
    shift = ((1.5**SCHULZ_STEPS) * half_way + mul(half_way, e3)) / scale
    shift = shift[0:1]
    transform = ((members - 1.0) ** 0.5 * root + shift).astype(BF16)

    inner_lane = lax.broadcasted_iota(jnp.int32, (1, LANES), 1)

    def interior(wide_value):
        fields = []
        for f in range(2):
            low = wide_value[:, f * LANES : (f + 1) * LANES]
            high = wide_value[:, (2 + f) * LANES : (3 + f) * LANES]
            fields.append(
                jnp.where(inner_lane % 8 < 4, lane_roll(low, -4), lane_roll(high, 4))
            )
        centre = (inner_lane >= 32) & (inner_lane < 96)
        return jnp.where(centre, fields[0], lane_roll(fields[1], 64))

    increment = jnp.dot(transform, inner, preferred_element_type=F32)
    inner_mean = interior(jnp.broadcast_to(mean, (8, 4 * LANES)))[0:1]
    top = top_lanes((8, LANES))
    mean_rows = jnp.broadcast_to(inner_mean, (8, LANES))
    turned_mean = jnp.where(top, lane_roll(mean_rows, -32), lane_roll(mean_rows, 32))[0:1]
    analysis = inner_mean + increment[:, :LANES]
    turned = turned_mean + increment[:, LANES:]
    parts = (n_mem, 2, 8, LANES)
    first, second = analysis.reshape(parts)[:, 0], turned.reshape(parts)[:, 1]
    top = top_lanes(first.shape)
    edges_up[...] = jnp.where(top, first, second).astype(BF16)
    edges_down[...] = jnp.where(top, second, first).astype(BF16)

    for partner in partners + [me_mem]:
        remote(
            edges_down.at[partner], above_part.at[me_mem], down_send, down_recv, partner, below
        ).start()
        remote(
            edges_up.at[partner], below_part.at[me_mem], up_send, up_recv, partner, above
        ).start()
    back_unit[...], grain = unit_of([analysis])
    scaled = (analysis * grain).reshape(parts)
    analysed[...] = pair_codes(scaled[:, 0], scaled[:, 1])
    for partner in partners:
        remote(
            analysed.at[partner], own_part.at[me_mem], own_send, own_recv, partner, me_row
        ).start()
    for partner in partners:
        remote(
            back_unit, back_units.at[me_mem], back_send, back_recv, partner, me_row
        ).start()
    own_part[me_mem] = analysed[me_mem]
    back_units[me_mem] = back_unit[...]
    for copy in band_copies[0] + band_copies[1] + obs_copies:
        copy.wait_send()
    region_all.wait_send()
    unit_all.wait_send()
    down_all = whole(above_part, n_mem, down_send, down_recv)
    up_all = whole(below_part, n_mem, up_send, up_recv)
    own_all = whole(own_part, others, own_send, own_recv)
    back_all = whole(back_units, others, back_send, back_recv)
    own_all.wait_recv()
    back_all.wait_recv()
    source = lax.broadcasted_iota(jnp.int32, (n_mem, LANES), 0)
    lane = lax.broadcasted_iota(jnp.int32, (n_mem, LANES), 1)
    unit_row = jnp.sum(
        jnp.where(lane // 8 == source, back_units[...].reshape(n_mem, LANES), 0.0),
        0,
        keepdims=True,
    )
    own_tiles = [
        jnp.concatenate([v * unit_row for v in codes_of(tile)], 0)
        for tile in swap_chunks([own_part[j] for j in range(n_mem)])
    ]
    state = [{} for _ in range(FSTEPS + 1)]
    state[0] = {i: (own_tiles[4 + i], own_tiles[(12 + i) % 16]) for i in range(PATCH)}

    def fill(first, last):
        for step in range(1, FSTEPS + 1):
            before, after = state[step - 1], state[step]
            for r in range(first + step, last - step):
                if r not in after:
                    after[r] = advance(before[r - 1], before[r], before[r + 1])

    fill(0, PATCH)
    down_all.wait_recv()
    up_all.wait_recv()
    edge_tiles = swap_chunks(
        [
            jnp.concatenate([below_part[j].astype(F32), above_part[j].astype(F32)], 0)
            for j in range(n_mem)
        ]
    )

    def edge_row(part, first, second):
        pick = slice(8 * part, 8 * part + 8)
        return jnp.concatenate([edge_tiles[first][pick], edge_tiles[second][pick]], 0)

    for i in range(RADIUS):
        state[0][i - RADIUS] = (edge_row(1, 8 + i, 4 + i), edge_row(1, i, 12 + i))
        state[0][i + PATCH] = (edge_row(0, 4 + i, 8 + i), edge_row(0, 12 + i, i))
    fill(-RADIUS, PATCH + RADIUS)
    for r in range(PATCH):
        for f in range(2):
            rows_of(out_ref, r, f)[...] = state[FSTEPS][r][f]

    for copies in (own_all, back_all, down_all, up_all):
        copies.wait_send()


def local(sample_collection, obs_values, obs_inverse_variance, obs_mask):
    n_mem, n_rows = lax.axis_size("mem"), lax.axis_size("rows")
    local_members = sample_collection.shape[0]
    dma = pltpu.SemaphoreType.DMA
    band = (2, PATCH, local_members // 2, LANES)
    flat = (local_members * 2 * PATCH, LANES)
    part = (n_mem, local_members // 2, LANES)
    result = pl.pallas_call(
        functools.partial(kernel, n_mem, n_rows),
        out_shape=pltpu.VMEM(flat, F32),
        in_specs=[pl.BlockSpec(memory_space=pl.ANY)] * 4,
        out_specs=pl.BlockSpec(memory_space=pltpu.VMEM),
        scratch_shapes=[
            pltpu.VMEM(flat, F32),
            pltpu.VMEM(obs_values.shape, F32),
            pltpu.VMEM(obs_values.shape, F32),
            pltpu.VMEM(obs_values.shape, jnp.int32),
        ]
        + [pltpu.VMEM(band, jnp.int32)] * 3
        + [pltpu.VMEM((8, LANES), F32)] * 6
        + [
            pltpu.VMEM((2, n_mem + 1, 8, LANES), jnp.int32),
            pltpu.VMEM((n_mem, 2, 2, 8, LANES), jnp.int32),
            pltpu.VMEM((2, 1, LANES), F32),
            pltpu.VMEM((n_mem, 2, 1, LANES), F32),
            pltpu.VMEM((1, LANES), F32),
            pltpu.VMEM((n_mem, 1, LANES), F32),
            pltpu.VMEM(part, jnp.int32),
            pltpu.VMEM(part, BF16),
            pltpu.VMEM(part, BF16),
            pltpu.VMEM(part, jnp.int32),
            pltpu.VMEM(part, BF16),
            pltpu.VMEM(part, BF16),
        ]
        + [pltpu.SemaphoreType.REGULAR]
        + [dma((4,)), dma((2, 2)), dma((2, 2)), dma((4,)), dma((4,))]
        + [dma(())] * 12,
        compiler_params=pltpu.CompilerParams(collective_id=0, has_side_effects=True),
    )(
        sample_collection.reshape(flat),
        obs_values,
        obs_inverse_variance,
        obs_mask,
    )
    return result.reshape(sample_collection.shape)


def solution(mesh):
    return jax.shard_map(
        local,
        mesh=mesh,
        in_specs=(
            P("mem", None, "rows", None),
            P(None, "rows", "mem"),
            P(None, "rows", "mem"),
            P(None, "rows", "mem"),
        ),
        out_specs=P("mem", None, "rows", None),
        check_vma=False,
    )
```
